128 devices in a mesh: lon: 16 (over y_lo, x, core), lat: 8 (over z, y_hi).
Axes of the slice: x: 4, y: 4 (y_hi: 2, y_lo: 2; y = y_hi * 2 + y_lo), z: 4, core: 2. Of those that a mesh axis runs over, the one named last changes fastest.
Arguments:
- courant_east: float32 [72, 512, 2048], P(None, 'lat', 'lon'), may hold values from -0.4 to 0.4
- courant_north: float32 [72, 512, 2048], P(None, 'lat', 'lon'), may hold values from -0.4 to 0.4
- obs_cells: int32 [8, 16, 1024], P('lat', 'lon'), may hold values from 0 to 8191
- misfit: float32 [5, 8, 16, 1024], P(None, 'lat', 'lon'), may hold values from -6 to 6
- kernel: float32 [72], replicated, may hold values from 0.25 to 1.75
- ensemble: bfloat16 [64, 512, 2048], P(None, 'lat', 'lon'), may hold values from -0.75 to 0.75
- pair_src: int32 [131072], P(('lon', 'lat')), may hold values from 0 to 4095
- pair_dst: int32 [131072], P(('lon', 'lat')), may hold values from 0 to 4095, as said below
- taper: float32 [131072], P(('lon', 'lat')), may hold values from 0.1 to 1
- var_scale: float32 [512, 2048], P('lat', 'lon'), may hold values from 0.3 to 3
Outputs:
- adjoint_field: float32 [72, 512, 2048], P(None, 'lat', 'lon')
- prior_grad: float32 [512, 2048], P('lat', 'lon')
The draws below stay inside these ranges and needn't reach their ends.
Inputs may be any that keep to these rules, and one draw needn't show every extreme that they name: `obs_cells`: each index names a cell of its own tile. `pair_dst`: block numbers; among the 1024 pairs of one device at most 64 name blocks of one tile, and some tile gets exactly 64 of them.
All inputs are finite; a program needn't handle non-finite values.
Results may differ from the reference program's by a relative error of at most 0.004.
Values sent between devices are 32-bit elements; how exact they have to be, the bound alone decides.
A program may use at most 128 MiB of HBM per device.

```python
import math
import jax
import jax.numpy as jnp
from jax import lax

TLAT = 64
TLON = 128
LEV = 72
STEPS = 4
BLK = 16
MEM = 64
OBS_DEV = 1024
PAIRS_DEV = 1024
ROUTE_CAP = 64
NLAT = 512
NLON = 2048
TILES_LAT = 8
TILES_LON = 16
NBLOCKS = 4096
NPAIRS = 131072
N_LON = 16
N_LAT = 8


def draw_pair_dst(key, part):
    own_count = TLAT // BLK * (TLON // BLK)
    owners = NBLOCKS // own_count
    devices_count = NPAIRS // PAIRS_DEV
    groups = PAIRS_DEV // ROUTE_CAP
    keys_owner = jax.random.split(jax.random.fold_in(key, 11), devices_count)
    keys_slot = jax.random.split(jax.random.fold_in(key, 12), devices_count)

    def one_device(key_owner, key_slot):
        chosen = jax.random.permutation(key_owner, owners)[:groups]
        order = jax.random.permutation(key_slot, PAIRS_DEV)
        return chosen[order // ROUTE_CAP]
    owner_of = jax.vmap(one_device)(keys_owner, keys_slot).reshape(-1)
    inner = jax.random.randint(jax.random.fold_in(key, 13), (NPAIRS,), 0, own_count)
    return (owner_of * own_count + inner).astype(jnp.int32)


def place_ends(drawn, own_key, least, top_value):
    longest = drawn.shape.index(max(drawn.shape))
    spots = []
    for shift in (0, 1):
        where = [jax.random.randint(jax.random.fold_in(own_key, axis), (), 0, length) for axis, length in enumerate(drawn.shape)]
        where[longest] = (where[longest] + shift) % drawn.shape[longest]
        spots.append(tuple(where))
    return drawn.at[spots[0]].set(least).at[spots[1]].set(top_value)


def steps_of(rng, extent, cuts, smallest, high):
    loudness = 1.0
    for dim, parts in cuts:
        heights = jax.random.uniform(jax.random.fold_in(jax.random.fold_in(rng, 6), dim), (parts,), jnp.float32, smallest / len(cuts), high / len(cuts))
        loudness = loudness * jnp.repeat(jnp.exp(heights), extent[dim] // parts).reshape((-1,) + (1,) * (len(extent) - 1 - dim))
    return loudness


def bell_draw(key, extent, deviation, limit, shards=(), kind=jnp.bfloat16):
    gain = steps_of(key, extent, shards, -0.22, 0.18) if shards else 1.0
    result = jax.random.normal(key, extent, jnp.float32) * deviation * gain
    return jnp.minimum(jnp.maximum(result, -limit), limit).astype(kind)


def setup_inputs(seed: int = 0) -> dict:
    arg_keys = jax.random.split(jax.random.key(seed), 11)
    return {
        "courant_east": jnp.clip(jax.random.uniform(arg_keys[0], (LEV, NLAT, NLON), jnp.float32, -0.4, 0.4) * steps_of(arg_keys[0], (LEV, NLAT, NLON), ((1, 8), (2, 16)), -0.4, 0.0), -0.4, 0.4),
        "courant_north": jnp.clip(jax.random.uniform(arg_keys[1], (LEV, NLAT, NLON), jnp.float32, -0.4, 0.4) * steps_of(arg_keys[1], (LEV, NLAT, NLON), ((1, 8), (2, 16)), -0.4, 0.0), -0.4, 0.4),
        "obs_cells": place_ends(jax.random.randint(arg_keys[2], (TILES_LAT, TILES_LON, OBS_DEV), 0, TLAT * TLON), jax.random.fold_in(arg_keys[2], 1), 0, (TLAT * TLON) - 1).astype(jnp.int32),
        "misfit": bell_draw(arg_keys[3], (STEPS + 1, TILES_LAT, TILES_LON, OBS_DEV), 1.0, 6.0, ((1, 8), (2, 16)), jnp.float32),
        "kernel": jnp.clip(1.0 + 0.15 * jax.random.normal(arg_keys[4], (LEV,), jnp.float32), 0.25, 1.75),
        "ensemble": bell_draw(arg_keys[5], (MEM, NLAT, NLON), 0.125, 0.75, ((1, 8), (2, 16))),
        "pair_src": place_ends(jax.random.randint(arg_keys[6], (NPAIRS,), 0, NBLOCKS), jax.random.fold_in(arg_keys[6], 1), 0, NBLOCKS - 1).astype(jnp.int32),
        "pair_dst": draw_pair_dst(jax.random.fold_in(arg_keys[10], 71), 0),
        "taper": jnp.clip(0.1 + 0.9 * jax.random.uniform(arg_keys[8], (NPAIRS,), jnp.float32) ** steps_of(arg_keys[8], (NPAIRS,), ((0, 128),), -0.2, 0.2), 0.1, 1.0),
        "var_scale": jnp.clip(jnp.exp(math.log(3.0) - 2.3025851 * jax.random.uniform(arg_keys[9], (NLAT, NLON), jnp.float32) ** steps_of(arg_keys[9], (NLAT, NLON), ((0, 8), (1, 16)), -0.2, 0.2)), 0.3, 3.0),
    }


def adjoint_apply(adj_field, pos_east, neg_west, pos_north, neg_south):
    east_vals = jnp.roll(adj_field, -1, axis=2)
    west_vals = jnp.roll(adj_field, 1, axis=2)
    padded = jnp.pad(adj_field, ((0, 0), (1, 1), (0, 0)))
    north_vals = padded[:, 2:, :]
    south_vals = padded[:, :-2, :]
    return (adj_field + pos_east * (east_vals - adj_field) + neg_west * (adj_field - west_vals)
            + pos_north * (north_vals - adj_field) + neg_south * (adj_field - south_vals))


def reference(courant_east, courant_north, obs_cells, misfit, kernel, ensemble, pair_src, pair_dst, taper, var_scale):
    north_face = courant_north.at[:, -1, :].set(0.0)
    pos_east = jnp.maximum(courant_east, 0.0)
    neg_west = jnp.roll(jnp.minimum(courant_east, 0.0), 1, axis=2)
    pos_north = jnp.maximum(north_face, 0.0)
    neg_south = jnp.pad(jnp.minimum(north_face, 0.0), ((0, 0), (1, 0), (0, 0)))[:, :-1, :]
    lat_rows = jnp.arange(N_LAT, dtype=jnp.int32)[:, None, None] * TLAT + obs_cells // TLON
    lon_cols = jnp.arange(N_LON, dtype=jnp.int32)[None, :, None] * TLON + obs_cells % TLON
    flat_cells = (lat_rows * NLON + lon_cols).reshape(-1)

    def forcing(step_index):
        column = jnp.zeros((NLAT * NLON,), jnp.float32).at[flat_cells].add(misfit[step_index].reshape(-1))
        return kernel[:, None, None] * column.reshape(NLAT, NLON)[None]

    adj_field = forcing(0)
    surface = adj_field[0]
    for step_index in range(1, STEPS + 1):
        adj_field = adjoint_apply(adj_field, pos_east, neg_west, pos_north, neg_south) + forcing(step_index)
        surface = surface + adj_field[0]
    block_rows = TLAT // BLK
    block_cols = TLON // BLK
    ens_blocks = ensemble.astype(jnp.float32).reshape(MEM, N_LAT, block_rows, BLK, N_LON, block_cols, BLK)
    rounded = lax.optimization_barrier(surface.astype(jnp.bfloat16)).astype(jnp.float32)
    grad_blocks = rounded.reshape(N_LAT, block_rows, BLK, N_LON, block_cols, BLK)
    coeffs = jnp.einsum("marpdcq,arpdcq->darcm", ens_blocks, grad_blocks).reshape(NBLOCKS, MEM)
    combined = jax.ops.segment_sum(taper[:, None] * coeffs[pair_src], pair_dst, num_segments=NBLOCKS)
    combined16 = lax.optimization_barrier(combined.astype(jnp.bfloat16)).astype(jnp.float32)
    combined16 = combined16.reshape(N_LON, N_LAT, block_rows, block_cols, MEM)
    field_part = jnp.einsum("marpdcq,darcm->arpdcq", ens_blocks, combined16).reshape(NLAT, NLON)
    prior_grad = var_scale * surface + field_part
    return adj_field, prior_grad
```

```python
import functools

import jax
import jax.numpy as jnp
from jax import lax
from jax.experimental import pallas as pl
from jax.experimental.pallas import tpu as pltpu
from jax.sharding import PartitionSpec as P

MESH = pl.DeviceIdType.MESH
F32, BF16, I32 = jnp.float32, jnp.bfloat16, jnp.int32

TLAT, TLON, LEV, BLK, MEM = 64, 128, 72, 16, 64
NLON, NLAT = 16, 8
FIELDS = 5
EXT = 7
ROWS = TLAT + 16
GROUPS = 3
KG = LEV // GROUPS
ROUNDS = 3
CHUNKS = 8
COPIES = 8 + 2 + 4 * ROUNDS * GROUPS + 15 + 7 + 1 + 9 + 9


def iota(shape, dim):
    return lax.broadcasted_iota(I32, shape, dim)


def dot_nt(a, b):
    return lax.dot_general(a, b, (((1,), (1,)), ((), ())), preferred_element_type=F32)


def dot_tn(a, b):
    return lax.dot_general(a, b, (((0,), (0,)), ((), ())), preferred_element_type=F32)


def dot_nn(a, b):
    return lax.dot_general(a, b, (((1,), (0,)), ((), ())), preferred_element_type=F32)


def parts_of(x, count):
    parts = []
    for _ in range(count):
        part = x.astype(BF16)
        parts.append(part)
        x = x - part.astype(F32)
    return parts


def kernel(
    ce_hbm, cn_hbm, cells, misfit, kern, ens_hbm, psrc, pdst, taper, var_ref,
    out_hbm, prior_ref,
    ce, cn, aw, asn, c0, field, last, ens, area, halo_e, halo_w, pack_e, pack_w,
    cpack, chalo, crow, crhalo, shifted,
    fpack_e, fpack_w, fhalo_e, fhalo_w, frow_n, frow_s, frhalo_n, frhalo_s,
    slots1, route1, slots2, route2, lhs, rhs, weights,
    partial, own, table, ycol,
    local_sem, out_sem, send_sem, recv_sem,
):
    lon, lat = lax.axis_index("lon"), lax.axis_index("lat")
    core, x, y_lo = lon % 2, (lon // 2) % 4, lon // 8
    z, y_hi = lat // 2, lat % 2
    y = y_hi * 2 + y_lo

    def shift_lon(s):
        return (lon + s + NLON) % NLON

    def shift_lat(s):
        return (lat + s + NLAT) % NLAT

    def device(xx, yy, zz, cc):
        return {"lon": (yy % 2) * 8 + xx * 2 + cc, "lat": zz * 2 + yy // 2}

    ce_in = pltpu.make_async_copy(ce_hbm, ce, local_sem.at[0])
    cn_in = pltpu.make_async_copy(cn_hbm, cn.at[:, pl.ds(8, TLAT), :], local_sem.at[1])
    ens_in = pltpu.make_async_copy(ens_hbm, ens, local_sem.at[2])
    ce_in.start()
    cn_in.start()
    ens_in.start()

    barrier = pltpu.get_barrier_semaphore()
    peers = [{"lon": shift_lon(i), "lat": lat} for i in range(1, NLON)]
    peers += [{"lon": lon, "lat": shift_lat(i)} for i in range(1, NLAT)]
    peers += [device(x, (y + i) % 4, z, core) for i in (1, 3)]
    peers += [{"lon": shift_lon(i), "lat": shift_lat(j)} for i in (-1, 1) for j in (-1, 1)]
    for peer in peers:
        pl.semaphore_signal(barrier, inc=1, device_id=peer, device_id_type=MESH)

    used = [0]

    def remote(src, dst, peer):
        n = used[0]
        used[0] += 1
        return pltpu.make_async_remote_copy(
            src_ref=src, dst_ref=dst, send_sem=send_sem.at[n], recv_sem=recv_sem.at[n],
            device_id=peer, device_id_type=MESH,
        )

    lane = iota((TLAT, TLON), 1)

    columns = [jnp.zeros((TLAT, TLON), F32) for _ in range(FIELDS)]
    for q in range(CHUNKS):
        cell = cells[q : q + 1, :]
        in_row = iota((TLAT, 128), 0) == cell // TLON
        in_col = jnp.where(iota((TLON, 128), 0) == cell % TLON, 1.0, 0.0).astype(BF16)
        weighted = []
        for t in range(FIELDS):
            value = misfit[t, q : q + 1, :]
            for part in parts_of(value, 2):
                weighted.append(jnp.where(in_row, part.astype(F32), 0.0).astype(BF16))
        placed = dot_nt(jnp.concatenate(weighted, axis=0), in_col)
        for t in range(FIELDS):
            base = 2 * t * TLAT
            columns[t] += placed[base : base + TLAT] + placed[base + TLAT : base + 2 * TLAT]
    for t in range(FIELDS):
        area[t, 8 : 8 + TLAT, :] = columns[t]

    total = jnp.zeros((128, 128), F32)
    slot1 = jnp.zeros((128, 128), F32)
    slot2 = jnp.zeros((128, 128), F32)
    before = jnp.where(iota((128, 128), 0) < iota((128, 128), 1), 1.0, 0.0).astype(BF16)
    ones = jnp.ones((128, 128), BF16)
    for q in range(CHUNKS):
        src, dst, weight = psrc[q : q + 1, :], pdst[q : q + 1, :], taper[q : q + 1, :]
        mine = iota((128, 128), 0) == dst // 32
        mark = jnp.where(mine, 1.0, 0.0).astype(BF16)
        count = dot_nn(mark, before) + total
        total += dot_nn(mark, ones)
        rank = jnp.sum(jnp.where(mine, count, 0.0), axis=0, keepdims=True).astype(I32)
        at_low = jnp.where(iota((128, 128), 0) == rank, 1.0, 0.0).astype(BF16)
        at_high = jnp.where(iota((128, 128), 0) == rank + 64, 1.0, 0.0).astype(BF16)
        s_tile, s_row, s_col = src // 32, (src // 8) % 4, src % 8
        s_lon, s_lat = s_tile // 8, s_tile % 8
        s_core, s_x, s_y, s_z = s_lon % 2, (s_lon // 2) % 4, (s_lat % 2) * 2 + s_lon // 8, s_lat // 2
        s_slot = jnp.where(s_core == 0, s_z * 16 + s_y * 4 + s_x, s_x * 16 + s_z * 4 + s_y)
        where_src = s_core * 512 + s_slot * 8 + s_col
        key1 = (where_src // 256) * 128 + s_row * 32 + dst % 32
        key2 = where_src % 256

        def spread(value):
            return jnp.where(mine, value, 0.0).astype(BF16)

        high, low = (key1 // 2 * 2).astype(F32), (key1 % 2).astype(F32)
        slot1 += dot_nt(spread(high), at_low) + dot_nt(spread(low), at_low)
        slot1 += dot_nt(spread(key2.astype(F32)), at_high)
        for part in parts_of(weight, 2):
            slot2 += dot_nt(spread(part.astype(F32)), at_low)
    for d in range(NLON):
        slots1[d, 0] = slot1[d * 8 : d * 8 + 8]
        slots1[d, 1] = slot2[d * 8 : d * 8 + 8]

    ce_in.wait()
    cn_in.wait()
    area[5, 8 : 8 + TLAT, :] = ce[0]
    area[6, 8 : 8 + TLAT, :] = cn[0, 8 : 8 + TLAT, :]
    first = jnp.zeros((TLAT, TLON), F32)
    final = jnp.zeros((TLAT, TLON), F32)
    for n in range(EXT):
        value = area[n, 8 : 8 + TLAT, :]
        here = (lane >= 4 * n) & (lane < 4 * n + 4)
        first = jnp.where(here, pltpu.roll(value, 4 * n, 1) if n else value, first)
        final = jnp.where(here, pltpu.roll(value, 4 * n + 4, 1), final)
    pack_w[...] = first
    pack_e[...] = final

    def pack_courant(k, acc):
        return jnp.where(lane == k, pltpu.roll(ce[k], k + 1, 1), acc)

    cpack[...] = lax.fori_loop(0, LEV, pack_courant, jnp.zeros((TLAT, TLON), F32))
    cn_rows = cn.reshape(LEV * (TLAT + 8), TLON)
    crow[...] = cn_rows[pl.ds(TLAT + 7, LEV, stride=TLAT + 8), :]

    pl.semaphore_wait(barrier, len(peers))

    east = {"lon": shift_lon(1), "lat": lat}
    west = {"lon": shift_lon(-1), "lat": lat}
    north = {"lon": lon, "lat": shift_lat(1)}
    south = {"lon": lon, "lat": shift_lat(-1)}
    mid, low8, high8 = pl.ds(8, TLAT), pl.ds(0, 8), pl.ds(TLAT + 8, 8)
    edges = [
        remote(area.at[:, pl.ds(TLAT, 8), :], area.at[:, low8, :], north),
        remote(area.at[:, pl.ds(8, 8), :], area.at[:, high8, :], south),
        remote(pack_e.at[pl.ds(TLAT - 8, 8), :], halo_w.at[low8, :], {"lon": shift_lon(1), "lat": shift_lat(1)}),
        remote(pack_e.at[pl.ds(0, 8), :], halo_w.at[high8, :], {"lon": shift_lon(1), "lat": shift_lat(-1)}),
        remote(pack_w.at[pl.ds(TLAT - 8, 8), :], halo_e.at[low8, :], {"lon": shift_lon(-1), "lat": shift_lat(1)}),
        remote(pack_w.at[pl.ds(0, 8), :], halo_e.at[high8, :], {"lon": shift_lon(-1), "lat": shift_lat(-1)}),
        remote(pack_e, halo_w.at[mid, :], east),
        remote(pack_w, halo_e.at[mid, :], west),
    ]
    courants = [remote(crow, crhalo, north), remote(cpack, chalo, east)]
    routes = [
        remote(slots1.at[shift_lon(i)], route1.at[lon], {"lon": shift_lon(i), "lat": lat})
        for i in range(1, NLON)
    ]
    for copy in edges + courants + routes:
        copy.start()

    for copy in edges:
        copy.wait_recv()

    wide_lane = iota((ROWS, TLON), 1)

    def widened(n):
        from_east = halo_e[...] if n == 0 else pltpu.roll(halo_e[...], 128 - 4 * n, 1)
        from_west = pltpu.roll(halo_w[...], 124 - 4 * n, 1)
        side = jnp.where(wide_lane < 64, from_east, from_west)
        return jnp.concatenate([area[n], side], axis=1)

    def up(v, axis):
        return pltpu.roll(v, v.shape[axis] - 1, axis)

    def down(v, axis):
        return pltpu.roll(v, 1, axis)

    forced = [widened(t) for t in range(FIELDS)]
    east0 = widened(5)
    global_row = lat * TLAT - 8 + iota((ROWS, 2 * TLON), 0)
    inside = (global_row >= 0) & (global_row < NLAT * TLAT - 1)
    north0 = jnp.where(inside, widened(6), 0.0)
    pe0, pn0 = jnp.maximum(east0, 0.0), jnp.maximum(north0, 0.0)
    aw0, as0 = -jnp.minimum(down(east0, 1), 0.0), -jnp.minimum(down(north0, 0), 0.0)
    c00 = 1.0 - pe0 - aw0 - pn0 - as0
    k0 = kern[0]
    level = k0 * forced[0]
    surface_wide = level
    for t in range(1, FIELDS):
        level = (
            c00 * level + pe0 * up(level, 1) + aw0 * down(level, 1)
            + pn0 * up(level, 0) + as0 * down(level, 0) + k0 * forced[t]
        )
        surface_wide = surface_wide + level
    surface = surface_wide[8 : 8 + TLAT, :TLON]
    prior_ref[...] = surface
    base = forced[0]
    for n, v in enumerate((base, up(base, 1), down(base, 1), up(base, 0), down(base, 0))):
        shifted[n] = v[8 : 8 + TLAT, :TLON]

    ens_in.wait()
    rounded = surface.astype(BF16).astype(F32)

    @pl.loop(0, MEM)
    def _(m):
        product = ens[m].astype(F32) * rounded
        for r in range(4):
            at = pl.multiple_of((r * MEM + m) * 8, 8)
            partial[pl.ds(at, 8), :] = product[r * 16 : r * 16 + 8] + product[r * 16 + 8 : r * 16 + 16]

    row_sums = partial[pl.ds(0, 256, stride=8), :]
    for s in range(1, 8):
        row_sums += partial[pl.ds(s, 256, stride=8), :]
    in_block = jnp.where(iota((8, TLON), 0) == iota((8, TLON), 1) // BLK, 1.0, 0.0).astype(BF16)
    own[...] = sum(dot_nt(in_block, part) for part in parts_of(row_sums, 3))

    slot = jnp.where(core == 0, z * 16 + y * 4 + x, x * 16 + z * 4 + y)
    sibling = device(x, y, z, 1 - core)
    moves = [(1 - core, core, 0), (0, 1 - core, core), (core, 0, 1 - core)]

    def ring_peer(phase, s):
        dx, dy, dz = moves[phase]
        return device((x + s * dx) % 4, (y + s * dy) % 4, (z + s * dz) % 4, core)

    def gather_sends(phase):
        if phase == 0:
            src, dst = own, table.at[core, slot]
        else:
            size = 4**phase
            first_slot = slot // size * size
            src = table.at[core, pl.ds(first_slot, size)]
            dst = table.at[core, pl.ds(first_slot, size)]
        return [remote(src, dst, ring_peer(phase, s)) for s in (2, 1, 3)]

    def share_sends(phase):
        size = 4**phase
        group = slot // (4 * size) * (4 * size)
        place = slot // size % 4
        copies = []
        for s in (1, 3, 2):
            rows = pl.ds(group + (place + s) % 4 * size, size)
            copies.append(remote(table.at[core, rows], table.at[core, rows], sibling))
        return copies

    shares = [remote(own, table.at[core, slot], sibling)]
    gathers = [gather_sends(0)]
    for copy in gathers[0] + shares:
        copy.start()
    table[core, slot] = own[...]

    def next_phase(phase):
        for copy in gathers[phase]:
            copy.wait_recv()
        if phase < 2:
            gathers.append(gather_sends(phase + 1))
            for copy in gathers[phase + 1]:
                copy.start()
        more = share_sends(phase)
        for copy in more:
            copy.start()
        shares.extend(more)

    for copy in courants:
        copy.wait_recv()
    cn_rows[pl.ds(7, LEV, stride=TLAT + 8), :] = crhalo[...] * jnp.where(lat > 0, 1.0, 0.0)
    field_rows = field.reshape(LEV * ROWS, TLON)
    keep = lat * TLAT + iota((TLAT, TLON), 0) < NLAT * TLAT - 1

    def step(t, g, k, carry):
        kk = kern[k]
        if t == 1:
            faces = ce[k]
            pe = jnp.maximum(faces, 0.0)
            behind = jnp.where(lane == 0, pltpu.roll(chalo[...], (128 - k) % 128, 1), pltpu.roll(faces, 1, 1))
            w = -jnp.minimum(behind, 0.0)
            pn = jnp.where(keep, jnp.maximum(cn[k, 8 : 8 + TLAT, :], 0.0), 0.0)
            s = -jnp.minimum(cn[k, 7 : 7 + TLAT, :], 0.0)
            c = 1.0 - pe - w - pn - s
            ce[k] = pe
            cn[k, 8 : 8 + TLAT, :] = pn
            aw[k], asn[k], c0[k] = w, s, c
            new = kk * (
                c * shifted[0] + pe * shifted[1] + w * shifted[2] + pn * shifted[3] + s * shifted[4]
                + area[1, 8 : 8 + TLAT, :]
            )
        else:
            here = field[k, 8 : 8 + TLAT, :]
            j = k - g * KG
            to_east = jnp.where(lane == 127, pltpu.roll(fhalo_e[t - 2, g], 127 - j, 1), pltpu.roll(here, 127, 1))
            to_west = jnp.where(lane == 0, pltpu.roll(fhalo_w[t - 2, g], (128 - j) % 128, 1), pltpu.roll(here, 1, 1))
            new = (
                c0[k] * here + ce[k] * to_east + aw[k] * to_west
                + cn[k, 8 : 8 + TLAT, :] * field[k, 9 : 9 + TLAT, :]
                + asn[k] * field[k, 7 : 7 + TLAT, :] + kk * area[t, 8 : 8 + TLAT, :]
            )
        if t == 4:
            last[k] = new
            return carry
        field[k, 8 : 8 + TLAT, :] = new
        j = k - g * KG
        first, final = carry
        first = jnp.where(lane == j, pltpu.roll(new, j, 1), first)
        final = jnp.where(lane == j, pltpu.roll(new, j + 1, 1), final)
        return first, final

    sent = {}
    outs = []

    def run_step(t):
        zeros = jnp.zeros((TLAT, TLON), F32)
        for g in range(GROUPS):
            start = g * KG * ROWS
            if t > 1:
                for copy in sent[t - 1, g]:
                    copy.wait_recv()
                field_rows[pl.ds(start + 7, KG, stride=ROWS), :] = frhalo_s[t - 2, g]
                field_rows[pl.ds(start + 8 + TLAT, KG, stride=ROWS), :] = frhalo_n[t - 2, g]
            if t == 4:
                lax.fori_loop(g * KG, (g + 1) * KG, functools.partial(step, t, g), 0)
                levels = pl.ds(g * KG, KG)
                outs.append(pltpu.make_async_copy(last.at[levels], out_hbm.at[levels], out_sem.at[g]))
                outs[-1].start()
                continue
            first, final = lax.fori_loop(
                g * KG, (g + 1) * KG, functools.partial(step, t, g), (zeros, zeros)
            )
            fpack_w[t - 1, g] = first
            fpack_e[t - 1, g] = final
            frow_n[t - 1, g] = field_rows[pl.ds(start + 7 + TLAT, KG, stride=ROWS), :]
            frow_s[t - 1, g] = field_rows[pl.ds(start + 8, KG, stride=ROWS), :]
            sent[t, g] = [
                remote(frow_n.at[t - 1, g], frhalo_s.at[t - 1, g], north),
                remote(frow_s.at[t - 1, g], frhalo_n.at[t - 1, g], south),
                remote(fpack_e.at[t - 1, g], fhalo_w.at[t - 1, g], east),
                remote(fpack_w.at[t - 1, g], fhalo_e.at[t - 1, g], west),
            ]
            for copy in sent[t, g]:
                copy.start()

    run_step(1)

    next_phase(0)

    route1[lon] = slots1[lon]
    for copy in routes:
        copy.wait_recv()
    for n in range(2):
        for a in range(NLAT):
            slots2[a, n] = jnp.concatenate([route1[d, n, a : a + 1, :] for d in range(NLON)], axis=0)
    routes2 = [
        remote(slots2.at[shift_lat(i)], route2.at[lat], {"lon": lon, "lat": shift_lat(i)})
        for i in range(1, NLAT)
    ]
    for copy in routes2:
        copy.start()
    route2[lat] = slots2[lat]

    run_step(2)

    next_phase(1)

    for copy in routes2:
        copy.wait_recv()
    half = iota((16, 128), 1) < 64

    for a in range(4):
        one, two = route2[a, 0], route2[a + 4, 0]
        key1 = jnp.where(half, one, pltpu.roll(two, 64, 1)).astype(I32)
        key2 = jnp.where(half, pltpu.roll(one, 64, 1), two).astype(I32)
        weight = jnp.where(half, route2[a, 1], pltpu.roll(route2[a + 4, 1], 64, 1))
        for q in range(2):
            for i in range(8):
                r = q * 8 + i
                cols = slice(i * 128, (i + 1) * 128)
                lhs[:, cols] = jnp.where(iota((512, 128), 0) == key1[r : r + 1], 1.0, 0.0).astype(BF16)
                match = iota((256, 128), 0) == key2[r : r + 1]
                high, low = parts_of(weight[r : r + 1], 2)
                rhs[:256, cols] = jnp.where(match, high.astype(F32), 0.0).astype(BF16)
                rhs[256:, cols] = jnp.where(match, low.astype(F32), 0.0).astype(BF16)
            both = dot_nt(lhs[...], rhs[...])
            if a == 0 and q == 0:
                weights[...] = both[:, :256] + both[:, 256:]
            else:
                weights[...] += both[:, :256] + both[:, 256:]

    run_step(3)

    next_phase(2)

    run_step(4)

    for copy in shares:
        copy.wait_recv()
    combined4 = jnp.zeros((128, 256), F32)
    for q in range(4):
        block = table[q // 2, (q % 2) * 32 : (q % 2) * 32 + 32].reshape(256, 256)
        t_high, t_low = parts_of(block, 2)
        w_high, w_low = parts_of(weights[q * 128 : (q + 1) * 128, :], 2)
        combined4 += dot_nn(w_high, t_high) + dot_nn(w_high, t_low) + dot_nn(w_low, t_high)
    combined = combined4[:32, :64]
    for r in range(1, 4):
        combined += combined4[r * 32 : (r + 1) * 32, r * 64 : (r + 1) * 64]
    for r in range(4):
        ycol[r] = dot_tn(combined[r * 8 : r * 8 + 8].astype(BF16), in_block)

    def add_member(m, acc):
        rows = [jnp.broadcast_to(ycol[r, pl.ds(m, 1), :], (BLK, TLON)) for r in range(4)]
        return acc + ens[m].astype(F32) * jnp.concatenate(rows, axis=0)

    prior_ref[...] = lax.fori_loop(0, MEM, add_member, var_ref[...] * prior_ref[...])

    for copy in outs:
        copy.wait()
    flights = edges + courants + routes + routes2 + shares
    flights += [copy for group in gathers for copy in group]
    flights += [copy for group in sent.values() for copy in group]
    for copy in flights:
        copy.wait_send()


def per_device(ce, cn, cells, misfit, kern, ens, psrc, pdst, taper, var):
    vmem = pl.BlockSpec(memory_space=pltpu.VMEM)
    hbm = pl.BlockSpec(memory_space=pl.ANY)
    tile = (TLAT, TLON)
    return pl.pallas_call(
        kernel,
        out_shape=(
            jax.ShapeDtypeStruct((LEV,) + tile, F32),
            jax.ShapeDtypeStruct(tile, F32),
        ),
        in_specs=[hbm, hbm, vmem, vmem, pl.BlockSpec(memory_space=pltpu.SMEM), hbm, vmem, vmem, vmem, vmem],
        out_specs=(hbm, vmem),
        scratch_shapes=[
            pltpu.VMEM((LEV,) + tile, F32),
            pltpu.VMEM((LEV, TLAT + 8, TLON), F32),
            pltpu.VMEM((LEV,) + tile, F32),
            pltpu.VMEM((LEV,) + tile, F32),
            pltpu.VMEM((LEV,) + tile, F32),
            pltpu.VMEM((LEV, ROWS, TLON), F32),
            pltpu.VMEM((LEV,) + tile, F32),
            pltpu.VMEM((MEM,) + tile, BF16),
            pltpu.VMEM((EXT, ROWS, TLON), F32),
            pltpu.VMEM((ROWS, TLON), F32),
            pltpu.VMEM((ROWS, TLON), F32),
            pltpu.VMEM(tile, F32),
            pltpu.VMEM(tile, F32),
            pltpu.VMEM(tile, F32),
            pltpu.VMEM(tile, F32),
            pltpu.VMEM((LEV, TLON), F32),
            pltpu.VMEM((LEV, TLON), F32),
            pltpu.VMEM((5,) + tile, F32),
        ]
        + [pltpu.VMEM((ROUNDS, GROUPS) + tile, F32) for _ in range(4)]
        + [pltpu.VMEM((ROUNDS, GROUPS, KG, TLON), F32) for _ in range(4)]
        + [
            pltpu.VMEM((NLON, 2, 8, 128), F32),
            pltpu.VMEM((NLON, 2, 8, 128), F32),
            pltpu.VMEM((NLAT, 2, 16, 128), F32),
            pltpu.VMEM((NLAT, 2, 16, 128), F32),
            pltpu.VMEM((512, 1024), BF16),
            pltpu.VMEM((512, 1024), BF16),
            pltpu.VMEM((512, 256), F32),
            pltpu.VMEM((256 * 8, TLON), F32),
            pltpu.VMEM((8, 256), F32),
            pltpu.VMEM((2, 64, 8, 256), F32),
            pltpu.VMEM((4, MEM, TLON), F32),
            pltpu.SemaphoreType.DMA((3,)),
            pltpu.SemaphoreType.DMA((GROUPS,)),
            pltpu.SemaphoreType.DMA((COPIES,)),
            pltpu.SemaphoreType.DMA((COPIES,)),
        ],
        compiler_params=pltpu.CompilerParams(
            collective_id=0, has_side_effects=True, vmem_limit_bytes=48 * 1024 * 1024
        ),
    )(
        ce, cn, cells.reshape(8, 128), misfit.reshape(FIELDS, 8, 128), kern, ens,
        psrc.reshape(8, 128), pdst.reshape(8, 128), taper.reshape(8, 128), var,
    )


def solution(mesh):
    in_specs = (
        P(None, "lat", "lon"),
        P(None, "lat", "lon"),
        P("lat", "lon", None),
        P(None, "lat", "lon", None),
        P(),
        P(None, "lat", "lon"),
        P(("lon", "lat")),
        P(("lon", "lat")),
        P(("lon", "lat")),
        P("lat", "lon"),
    )
    out_specs = (P(None, "lat", "lon"), P("lat", "lon"))
    return jax.shard_map(
        per_device, mesh=mesh, in_specs=in_specs, out_specs=out_specs, check_vma=False
    )
```

```python
import functools

import jax
import jax.numpy as jnp
from jax import lax
from jax.experimental import pallas as pl
from jax.experimental.pallas import tpu as pltpu
from jax.sharding import PartitionSpec as P

MESH = pl.DeviceIdType.MESH
F32, BF16, I32, I16 = jnp.float32, jnp.bfloat16, jnp.int32, jnp.int16

TLAT, TLON, LEV, BLK, MEM = 64, 128, 72, 16, 64
NLON, NLAT = 16, 8
FIELDS = 5
EXT = 7
ROWS = TLAT + 16
GROUPS = 3
PIECES = 8
KG = LEV // GROUPS
LEVELS = 24
ROUNDS = 3
CHUNKS = 8
COPIES = 8 + 2 + 4 * ROUNDS * GROUPS + 15 + 7 + 1 + 9 + 9


def iota(shape, dim):
    return lax.broadcasted_iota(I32, shape, dim)


def dot_nt(a, b):
    return lax.dot_general(a, b, (((1,), (1,)), ((), ())), preferred_element_type=F32)


def dot_tn(a, b):
    return lax.dot_general(a, b, (((0,), (0,)), ((), ())), preferred_element_type=F32)


def dot_nn(a, b):
    return lax.dot_general(a, b, (((1,), (0,)), ((), ())), preferred_element_type=F32)


def spread_row(row, dtype, rows):
    few = jnp.broadcast_to(row, (16, 128)).astype(dtype)
    return jnp.concatenate([few] * (rows // 16), axis=0)


def select(mask, row, rows):
    return jnp.where(mask, spread_row(row, BF16, rows), jnp.zeros((), BF16))


def one_hot(mask):
    return jnp.where(mask, jnp.ones((), BF16), jnp.zeros((), BF16))


def parts_of(x, count):
    parts = []
    for _ in range(count):
        part = x.astype(BF16)
        parts.append(part)
        x = x - part.astype(F32)
    return parts


def kernel(
    ce_hbm, cn_hbm, cells_hbm, misfit_hbm, kern_hbm, ens_hbm, psrc_hbm, pdst_hbm, taper_hbm, var_hbm,
    out_hbm, prior_hbm,
    cells, misfit, kern, psrc, pdst, taper, var_ref,
    ce, cn, aw, asn, c0, field, field16, last, ens, area, halo_e, halo_w, pack_e, pack_w,
    cpack, chalo, crow, crhalo, shifted,
    fpack, fhalo_e, fhalo_w, move, ends, every, to_first, frow_n, frow_s, frhalo_n, frhalo_s,
    slots1, route1, slots2, route2, keys, weights, weights16,
    partial, own, table, ycol, prior,
    local_sem, out_sem, send_sem, recv_sem,
):
    lon, lat = lax.axis_index("lon"), lax.axis_index("lat")
    core, x, y_lo = lon % 2, (lon // 2) % 4, lon // 8
    z, y_hi = lat // 2, lat % 2
    y = y_hi * 2 + y_lo

    def shift_lon(s):
        return (lon + s + NLON) % NLON

    def shift_lat(s):
        return (lat + s + NLAT) % NLAT

    def device(xx, yy, zz, cc):
        return {"lon": (yy % 2) * 8 + xx * 2 + cc, "lat": zz * 2 + yy // 2}

    rest = pl.ds(1, LEV - 1)
    ce_in = pltpu.make_async_copy(ce_hbm.at[rest], ce.at[rest], local_sem.at[0])
    cn_in = pltpu.make_async_copy(cn_hbm.at[rest], cn.at[rest, pl.ds(8, TLAT), :], local_sem.at[1])
    ens_in = pltpu.make_async_copy(ens_hbm, ens, local_sem.at[2])
    small = [
        pltpu.make_async_copy(src, dst, local_sem.at[3 + n])
        for n, (src, dst) in enumerate((
            (cells_hbm, cells), (misfit_hbm, misfit), (kern_hbm, kern), (psrc_hbm, psrc),
            (pdst_hbm, pdst), (taper_hbm, taper), (var_hbm, var_ref),
            (ce_hbm.at[0], ce.at[0]), (cn_hbm.at[0], cn.at[0, pl.ds(8, TLAT), :]),
        ))
    ]
    for copy in small + [ce_in, cn_in, ens_in]:
        copy.start()

    barrier = pltpu.get_barrier_semaphore()
    peers = [{"lon": shift_lon(i), "lat": lat} for i in range(1, NLON)]
    peers += [{"lon": lon, "lat": shift_lat(i)} for i in range(1, NLAT)]
    peers += [device(x, (y + i) % 4, z, core) for i in (1, 3)]
    peers += [{"lon": shift_lon(i), "lat": shift_lat(j)} for i in (-1, 1) for j in (-1, 1)]
    for peer in peers:
        pl.semaphore_signal(barrier, inc=1, device_id=peer, device_id_type=MESH)

    used = [0]

    def remote(src, dst, peer):
        n = used[0]
        used[0] += 1
        return pltpu.make_async_remote_copy(
            src_ref=src, dst_ref=dst, send_sem=send_sem.at[n], recv_sem=recv_sem.at[n],
            device_id=peer, device_id_type=MESH,
        )

    lane = iota((TLAT, TLON), 1)
    lane32 = lane % 32

    row, col = iota((256, 256), 0), iota((256, 256), 1)
    shift = (row < 128) & (((col < 128) & (row == col + 1)) | ((col >= 128) & (row + 129 == col)))
    edge = ((row >= 160) & (row < 192) & (col == 127)) | ((row >= 128) & (row < 160) & (col == 128))
    move[...] = jnp.where(shift | edge, 1.0, 0.0).astype(BF16)
    end = ((row % 128 == 127) & (col % 128 < 32)) | ((row % 128 == 0) & (col % 128 >= 32) & (col % 128 < 64))
    end = end & (row // 128 == col // 128)
    ends[...] = jnp.where(end, 1.0, 0.0).astype(BF16)
    row, col = iota((128, 128), 0), iota((128, 128), 1)
    every[...] = jnp.where(row == 127, 1.0, 0.0).astype(BF16)
    to_first[...] = jnp.where(col == 0, 1.0, 0.0).astype(BF16)

    for copy in small:
        copy.wait()

    columns = [jnp.zeros((TLAT, TLON), F32) for _ in range(FIELDS)]
    cell_row, cell_col = cells[...] >> 7, cells[...] & 127
    number = iota((128, 128), 0).astype(I16)
    for q in range(CHUNKS):
        in_row = number[:TLAT] == spread_row(cell_row[q : q + 1], I16, TLAT)
        in_col = one_hot(number == spread_row(cell_col[q : q + 1], I16, TLON))
        weighted = []
        for t in range(FIELDS):
            for part in parts_of(misfit[t, q : q + 1, :], 2):
                weighted.append(select(in_row, part.astype(F32), TLAT))
        placed = dot_nt(jnp.concatenate(weighted, axis=0), in_col)
        for t in range(FIELDS):
            base = 2 * t * TLAT
            columns[t] += placed[base : base + TLAT] + placed[base + TLAT : base + 2 * TLAT]
    for t in range(FIELDS):
        area[t, 8 : 8 + TLAT, :] = columns[t]

    area[5, 8 : 8 + TLAT, :] = ce[0]
    area[6, 8 : 8 + TLAT, :] = cn[0, 8 : 8 + TLAT, :]
    first = jnp.zeros((TLAT, TLON), F32)
    final = jnp.zeros((TLAT, TLON), F32)
    for n in range(EXT):
        value = area[n, 8 : 8 + TLAT, :]
        here = (lane >= 4 * n) & (lane < 4 * n + 4)
        first = jnp.where(here, pltpu.roll(value, 4 * n, 1) if n else value, first)
        final = jnp.where(here, pltpu.roll(value, 4 * n + 4, 1), final)
    pack_w[...] = first
    pack_e[...] = final

    pl.semaphore_wait(barrier, len(peers))

    east = {"lon": shift_lon(1), "lat": lat}
    west = {"lon": shift_lon(-1), "lat": lat}
    north = {"lon": lon, "lat": shift_lat(1)}
    south = {"lon": lon, "lat": shift_lat(-1)}
    mid, low8, high8 = pl.ds(8, TLAT), pl.ds(0, 8), pl.ds(TLAT + 8, 8)
    edges = [
        remote(area.at[:, pl.ds(TLAT, 8), :], area.at[:, low8, :], north),
        remote(area.at[:, pl.ds(8, 8), :], area.at[:, high8, :], south),
        remote(pack_e.at[pl.ds(TLAT - 8, 8), :], halo_w.at[low8, :], {"lon": shift_lon(1), "lat": shift_lat(1)}),
        remote(pack_e.at[pl.ds(0, 8), :], halo_w.at[high8, :], {"lon": shift_lon(1), "lat": shift_lat(-1)}),
        remote(pack_w.at[pl.ds(TLAT - 8, 8), :], halo_e.at[low8, :], {"lon": shift_lon(-1), "lat": shift_lat(1)}),
        remote(pack_w.at[pl.ds(0, 8), :], halo_e.at[high8, :], {"lon": shift_lon(-1), "lat": shift_lat(-1)}),
        remote(pack_e, halo_w.at[mid, :], east),
        remote(pack_w, halo_e.at[mid, :], west),
    ]
    for copy in edges:
        copy.start()

    ce_in.wait()

    def pack_courant(kb, acc):
        faces = [ce[kb * 8 + i].astype(BF16) for i in range(8)]
        tips = dot_nn(jnp.concatenate(faces, axis=0), every[...])
        for i in range(8):
            acc = jnp.where(lane == kb * 8 + i, tips[i * TLAT : (i + 1) * TLAT], acc)
        return acc

    cpack[...] = lax.fori_loop(0, LEV // 8, pack_courant, jnp.zeros((TLAT, TLON), F32))
    cn_in.wait()
    cn_rows = cn.reshape(LEV * (TLAT + 8), TLON)
    last_row = cn_rows[pl.ds(TLAT + 7, LEV, stride=TLAT + 8), :] * jnp.where(lat < NLAT - 1, 1.0, 0.0)
    crow[...] = last_row
    cn_rows[pl.ds(TLAT + 7, LEV, stride=TLAT + 8), :] = last_row
    courants = [remote(crow, crhalo, north), remote(cpack, chalo, east)]
    for copy in courants:
        copy.start()

    total = jnp.zeros((128, 128), F32)
    slot1 = jnp.zeros((128, 128), F32)
    slot2 = jnp.zeros((128, 128), F32)
    before = jnp.where(iota((128, 128), 0) < iota((128, 128), 1), 1.0, 0.0).astype(BF16)
    ones = jnp.ones((128, 128), BF16)
    src, dst = psrc[...], pdst[...]
    s_lon, s_lat = src >> 8, (src >> 5) & 7
    s_x, s_y, s_z = (s_lon >> 1) & 3, (s_lat & 1) * 2 + (s_lon >> 3), s_lat >> 1
    s_slot = jnp.where((s_lon & 1) == 0, s_z * 16 + s_y * 4 + s_x, s_x * 16 + s_z * 4 + s_y)
    key1 = ((s_lon & 1) * 128 + ((src >> 3) & 3) * 32 + (dst & 31)).astype(F32)
    key2_high, key2_low = (s_slot * 8).astype(F32), (src & 7).astype(F32)
    tile = dst >> 5
    for q in range(CHUNKS):
        at = slice(q, q + 1)
        here = iota((128, 128), 0) == tile[at]
        mine = number == spread_row(tile[at], I16, 128)
        mark = one_hot(mine)
        count = dot_nn(mark, before) + total
        total += dot_nn(mark, ones)
        rank = jnp.sum(jnp.where(here, count, 0.0), axis=0, keepdims=True).astype(I32)
        at_low = one_hot(number == spread_row(rank, I16, 128))
        at_high = one_hot(number == spread_row(rank + 64, I16, 128))
        slot1 += dot_nt(select(mine, key1[at], 128), at_low)
        slot1 += dot_nt(select(mine, key2_high[at], 128), at_high)
        slot1 += dot_nt(select(mine, key2_low[at], 128), at_high)
        slot2 += dot_nt(select(mine, taper[at, :], 128), at_low)
    for d in range(NLON):
        slots1[d, 0] = slot1[d * 8 : d * 8 + 8]
        slots1[d, 1] = slot2[d * 8 : d * 8 + 8]

    routes = [
        remote(slots1.at[shift_lon(i)], route1.at[lon], {"lon": shift_lon(i), "lat": lat})
        for i in range(1, NLON)
    ]
    for copy in routes:
        copy.start()

    for copy in edges:
        copy.wait_recv()

    wide_lane = iota((ROWS, TLON), 1)

    def widened(n):
        from_east = halo_e[...] if n == 0 else pltpu.roll(halo_e[...], 128 - 4 * n, 1)
        from_west = pltpu.roll(halo_w[...], 124 - 4 * n, 1)
        side = jnp.where(wide_lane < 64, from_east, from_west)
        return jnp.concatenate([area[n], side], axis=1)

    def up(v, axis):
        return pltpu.roll(v, v.shape[axis] - 1, axis)

    def down(v, axis):
        return pltpu.roll(v, 1, axis)

    forced = [widened(t) for t in range(FIELDS)]
    east0 = widened(5)
    global_row = lat * TLAT - 8 + iota((ROWS, 2 * TLON), 0)
    inside = (global_row >= 0) & (global_row < NLAT * TLAT - 1)
    north0 = jnp.where(inside, widened(6), 0.0)
    pe0, pn0 = jnp.maximum(east0, 0.0), jnp.maximum(north0, 0.0)
    aw0, as0 = -jnp.minimum(down(east0, 1), 0.0), -jnp.minimum(down(north0, 0), 0.0)
    c00 = 1.0 - pe0 - aw0 - pn0 - as0
    k0 = kern[0]
    level = k0 * forced[0]
    surface_wide = level
    for t in range(1, FIELDS):
        level = (
            c00 * level + pe0 * up(level, 1) + aw0 * down(level, 1)
            + pn0 * up(level, 0) + as0 * down(level, 0) + k0 * forced[t]
        )
        surface_wide = surface_wide + level
    surface = surface_wide[8 : 8 + TLAT, :TLON]
    prior[...] = surface
    base = forced[0]
    for n, v in enumerate((base, up(base, 1), down(base, 1), up(base, 0), down(base, 0))):
        shifted[n] = v[8 : 8 + TLAT, :TLON]

    ens_in.wait()
    rounded = surface.astype(BF16).astype(F32)

    @pl.loop(0, MEM)
    def _(m):
        product = ens[m].astype(F32) * rounded
        for r in range(4):
            at = pl.multiple_of((r * MEM + m) * 8, 8)
            partial[pl.ds(at, 8), :] = product[r * 16 : r * 16 + 8] + product[r * 16 + 8 : r * 16 + 16]

    row_sums = partial[pl.ds(0, 256, stride=8), :]
    for s in range(1, 8):
        row_sums += partial[pl.ds(s, 256, stride=8), :]
    in_block = jnp.where(iota((8, TLON), 0) == iota((8, TLON), 1) // BLK, 1.0, 0.0).astype(BF16)
    own[...] = sum(dot_nt(in_block, part) for part in parts_of(row_sums, 3))

    slot = jnp.where(core == 0, z * 16 + y * 4 + x, x * 16 + z * 4 + y)
    sibling = device(x, y, z, 1 - core)
    moves = [(1 - core, core, 0), (0, 1 - core, core), (core, 0, 1 - core)]

    def ring_peer(phase, s):
        dx, dy, dz = moves[phase]
        return device((x + s * dx) % 4, (y + s * dy) % 4, (z + s * dz) % 4, core)

    def gather_sends(phase):
        if phase == 0:
            src, dst = own, table.at[core, slot]
        else:
            size = 4**phase
            first_slot = slot // size * size
            src = table.at[core, pl.ds(first_slot, size)]
            dst = table.at[core, pl.ds(first_slot, size)]
        return [remote(src, dst, ring_peer(phase, s)) for s in (2, 1, 3)]

    def share_sends(phase):
        size = 4**phase
        group = slot // (4 * size) * (4 * size)
        place = slot // size % 4
        copies = []
        for s in (1, 3, 2):
            rows = pl.ds(group + (place + s) % 4 * size, size)
            copies.append(remote(table.at[core, rows], table.at[core, rows], sibling))
        return copies

    shares = [remote(own, table.at[core, slot], sibling)]
    gathers = [gather_sends(0)]
    for copy in gathers[0] + shares:
        copy.start()
    table[core, slot] = own[...]

    def next_phase(phase):
        for copy in gathers[phase]:
            copy.wait_recv()
        if phase < 2:
            gathers.append(gather_sends(phase + 1))
            for copy in gathers[phase + 1]:
                copy.start()
        more = share_sends(phase)
        for copy in more:
            copy.start()
        shares.extend(more)

    for copy in courants:
        copy.wait_recv()
    cn_rows[pl.ds(7, LEV, stride=TLAT + 8), :] = crhalo[...] * jnp.where(lat > 0, 1.0, 0.0)
    field_rows = field.reshape(LEV * ROWS, TLON)

    def block(t, g, halo, kb, pack):
        base = g * KG + kb * LEVELS
        if t > 1:
            rows = []
            for i in range(LEVELS):
                mine = jnp.where(lane32 == kb * LEVELS + i, halo, 0.0).astype(BF16)
                rows.append(jnp.concatenate([field16[base + i], mine], axis=1))
            moved = dot_nn(jnp.concatenate(rows, axis=0), move[...])
        else:
            rows = [jnp.where(lane == base + i, halo, 0.0).astype(BF16) for i in range(LEVELS)]
            moved = dot_nn(jnp.concatenate(rows, axis=0), to_first[...])
        rounded = []
        for i in range(LEVELS):
            k = base + i
            kk = kern[k]
            if t == 1:
                faces = ce[k]
                pe = jnp.maximum(faces, 0.0)
                behind = jnp.where(lane == 0, moved[i * TLAT : (i + 1) * TLAT], pltpu.roll(faces, 1, 1))
                w = jnp.minimum(behind, 0.0)
                pn = jnp.maximum(cn[k, 8 : 8 + TLAT, :], 0.0)
                s = jnp.minimum(cn[k, 7 : 7 + TLAT, :], 0.0)
                c = (1.0 - pe) + w - pn + s
                ce[k] = pe
                cn[k, 8 : 8 + TLAT, :] = pn
                aw[k], asn[k], c0[k] = w, s, c
                new = kk * (
                    c * shifted[0] + pe * shifted[1] - w * shifted[2] + pn * shifted[3] - s * shifted[4]
                    + area[1, 8 : 8 + TLAT, :]
                )
            else:
                level_rows = slice(i * TLAT, (i + 1) * TLAT)
                new = (
                    c0[k] * field[k, 8 : 8 + TLAT, :]
                    + ce[k] * moved[level_rows, :TLON] - aw[k] * moved[level_rows, TLON:]
                    + cn[k, 8 : 8 + TLAT, :] * field[k, 9 : 9 + TLAT, :]
                    - asn[k] * field[k, 7 : 7 + TLAT, :] + kk * area[t, 8 : 8 + TLAT, :]
                )
            if t == 4:
                last[k] = new
                continue
            field[k, 8 : 8 + TLAT, :] = new
            new16 = new.astype(BF16)
            field16[k] = new16
            rounded.append(new16)
        if t == 4:
            return pack
        pairs = [jnp.concatenate(rounded[i : i + 2], axis=1) for i in range(0, LEVELS, 2)]
        tips = dot_nn(jnp.concatenate(pairs, axis=0), ends[...])
        for i in range(LEVELS):
            tip = tips[i // 2 * TLAT : (i // 2 + 1) * TLAT, i % 2 * TLON : (i % 2 + 1) * TLON]
            pack = jnp.where(lane32 == kb * LEVELS + i, tip, pack)
        return pack

    sent = {}
    outs = []

    def run_group(t, g):
        start = g * KG * ROWS
        halo = chalo[...]
        if t > 1:
            for copy in sent[t - 1, g]:
                copy.wait_recv()
            field_rows[pl.ds(start + 7, KG, stride=ROWS), :] = frhalo_s[t - 2, g]
            field_rows[pl.ds(start + 8 + TLAT, KG, stride=ROWS), :] = frhalo_n[t - 2, g]
            halo = jnp.where(lane < 32, fhalo_w[t - 2, g], fhalo_e[t - 2, g])
        run = functools.partial(block, t, g, halo)
        pack = lax.fori_loop(0, KG // LEVELS, run, 0 if t == 4 else jnp.zeros((TLAT, TLON), F32))
        if t == 4:
            levels = pl.ds(g * KG, KG)
            outs.append(pltpu.make_async_copy(last.at[levels], out_hbm.at[levels], out_sem.at[g]))
            outs[-1].start()
            return
        fpack[t - 1, g] = pack
        frow_n[t - 1, g] = field_rows[pl.ds(start + 7 + TLAT, KG, stride=ROWS), :]
        frow_s[t - 1, g] = field_rows[pl.ds(start + 8, KG, stride=ROWS), :]
        sent[t, g] = [
            remote(frow_n.at[t - 1, g], frhalo_s.at[t - 1, g], north),
            remote(frow_s.at[t - 1, g], frhalo_n.at[t - 1, g], south),
            remote(fpack.at[t - 1, g], fhalo_w.at[t - 1, g], east),
            remote(fpack.at[t - 1, g], fhalo_e.at[t - 1, g], west),
        ]
        for copy in sent[t, g]:
            copy.start()

    run_group(1, 0)

    route1[lon] = slots1[lon]
    for copy in routes:
        copy.wait_recv()
    for n in range(2):
        for a in range(NLAT):
            slots2[a, n] = jnp.concatenate([route1[d, n, a : a + 1, :] for d in range(NLON)], axis=0)
    routes2 = [
        remote(slots2.at[shift_lat(i)], route2.at[lat], {"lon": lon, "lat": shift_lat(i)})
        for i in range(1, NLAT)
    ]
    for copy in routes2:
        copy.start()
    route2[lat] = slots2[lat]

    run_group(1, 1)
    next_phase(0)
    run_group(1, 2)

    run_group(2, 0)
    run_group(2, 1)
    next_phase(1)
    run_group(2, 2)

    for copy in routes2:
        copy.wait_recv()
    half = iota((16, 128), 1) < 64
    for a in range(4):
        one, two = route2[a, 0], route2[a + 4, 0]
        at = slice(a * 16, a * 16 + 16)
        keys[0, at] = jnp.where(half, one, pltpu.roll(two, 64, 1))
        keys[1, at] = jnp.where(half, pltpu.roll(one, 64, 1), two)
        keys[2, at] = jnp.where(half, route2[a, 1], pltpu.roll(route2[a + 4, 1], 64, 1))
    weights[...] = jnp.zeros_like(weights)

    def add_weights(i, carry):
        at = pl.ds(pl.multiple_of(i * 8, 8), 8)
        key1, key2, weight = keys[0, at, :].astype(I32), keys[1, at, :].astype(I32), keys[2, at, :]
        number = iota((128, 128), 0).astype(I16)
        lhs, rhs = [], []
        for u in range(8):
            one = slice(u, u + 1)
            match = [number == spread_row(key1[one] - r, I16, 128) for r in (0, 128)]
            lhs.append(jnp.concatenate([select(m, weight[one], 128) for m in match], axis=0))
            match = [number == spread_row(key2[one] - r, I16, 128) for r in (0, 128, 256, 384)]
            rhs.append(jnp.concatenate([one_hot(m) for m in match], axis=0))
        weights[...] += dot_nt(jnp.concatenate(lhs, axis=1), jnp.concatenate(rhs, axis=1))
        return carry

    lax.fori_loop(0, 4, add_weights, 0)

    run_group(3, 0)
    run_group(3, 1)
    next_phase(2)
    run_group(3, 2)

    lax.fori_loop(4, 8, add_weights, 0)
    w_parts = parts_of(weights[...], 2)
    weights16[0] = w_parts[0]
    weights16[1] = w_parts[1]

    run_group(4, 0)

    for copy in shares:
        copy.wait_recv()
    combined4 = jnp.zeros((128, 256), F32)
    for q in range(4):
        table_part = table[q // 2, (q % 2) * 32 : (q % 2) * 32 + 32].reshape(256, 256)
        t_high, t_low = parts_of(table_part, 2)
        w_rows, w_cols = slice(q // 2 * 128, q // 2 * 128 + 128), slice(q % 2 * 256, q % 2 * 256 + 256)
        w_high, w_low = weights16[0, w_rows, w_cols], weights16[1, w_rows, w_cols]
        combined4 += dot_nn(w_high, t_high) + dot_nn(w_high, t_low) + dot_nn(w_low, t_high)
    combined = combined4[:32, :64]
    for r in range(1, 4):
        combined += combined4[r * 32 : (r + 1) * 32, r * 64 : (r + 1) * 64]
    for r in range(4):
        ycol[r] = dot_tn(combined[r * 8 : r * 8 + 8].astype(BF16), in_block)

    def add_member(m, acc):
        rows = [jnp.broadcast_to(ycol[r, pl.ds(m, 1), :], (BLK, TLON)) for r in range(4)]
        return acc + ens[m].astype(F32) * jnp.concatenate(rows, axis=0)

    prior[...] = lax.fori_loop(0, MEM, add_member, var_ref[...] * prior[...], unroll=8)
    outs.append(pltpu.make_async_copy(prior, prior_hbm, out_sem.at[GROUPS]))
    outs[-1].start()

    run_group(4, 1)
    run_group(4, 2)

    for copy in outs:
        copy.wait()
    flights = edges + courants + routes + routes2 + shares
    flights += [copy for group in gathers for copy in group]
    flights += [copy for group in sent.values() for copy in group]
    for copy in flights:
        copy.wait_send()


def hand_over(field, prior, field_out, prior_out, field_held, prior_held, in_sem, out_sem):
    steps = LEV // PIECES
    parts = [(prior, prior_held, prior_out)]
    for n in range(PIECES):
        levels = pl.ds(n * steps, steps)
        parts.append((field.at[levels], field_held.at[levels], field_out.at[levels]))
    loads = [
        pltpu.make_async_copy(src, held, in_sem.at[n]) for n, (src, held, _) in enumerate(parts)
    ]
    stores = [
        pltpu.make_async_copy(held, dst, out_sem.at[n]) for n, (_, held, dst) in enumerate(parts)
    ]
    for load in loads:
        load.start()
    for load, store in zip(loads, stores):
        load.wait()
        store.start()
    for store in stores:
        store.wait()


def per_device(ce, cn, cells, misfit, kern, ens, psrc, pdst, taper, var):
    hbm = pl.BlockSpec(memory_space=pl.ANY)
    tile = (TLAT, TLON)
    field, prior = pl.pallas_call(
        kernel,
        out_shape=(
            jax.ShapeDtypeStruct((LEV,) + tile, F32),
            jax.ShapeDtypeStruct(tile, F32),
        ),
        in_specs=[hbm] * 10,
        out_specs=(hbm, hbm),
        scratch_shapes=[
            pltpu.VMEM((8, 128), I32),
            pltpu.VMEM((FIELDS, 8, 128), F32),
            pltpu.SMEM((LEV,), F32),
            pltpu.VMEM((8, 128), I32),
            pltpu.VMEM((8, 128), I32),
            pltpu.VMEM((8, 128), F32),
            pltpu.VMEM(tile, F32),
            pltpu.VMEM((LEV,) + tile, F32),
            pltpu.VMEM((LEV, TLAT + 8, TLON), F32),
            pltpu.VMEM((LEV,) + tile, F32),
            pltpu.VMEM((LEV,) + tile, F32),
            pltpu.VMEM((LEV,) + tile, F32),
            pltpu.VMEM((LEV, ROWS, TLON), F32),
            pltpu.VMEM((LEV,) + tile, BF16),
            pltpu.VMEM((LEV,) + tile, F32),
            pltpu.VMEM((MEM,) + tile, BF16),
            pltpu.VMEM((EXT, ROWS, TLON), F32),
            pltpu.VMEM((ROWS, TLON), F32),
            pltpu.VMEM((ROWS, TLON), F32),
            pltpu.VMEM(tile, F32),
            pltpu.VMEM(tile, F32),
            pltpu.VMEM(tile, F32),
            pltpu.VMEM(tile, F32),
            pltpu.VMEM((LEV, TLON), F32),
            pltpu.VMEM((LEV, TLON), F32),
            pltpu.VMEM((5,) + tile, F32),
        ]
        + [pltpu.VMEM((ROUNDS, GROUPS) + tile, F32) for _ in range(3)]
        + [pltpu.VMEM((256, 256), BF16) for _ in range(2)]
        + [pltpu.VMEM((128, 128), BF16) for _ in range(2)]
        + [pltpu.VMEM((ROUNDS, GROUPS, KG, TLON), F32) for _ in range(4)]
        + [
            pltpu.VMEM((NLON, 2, 8, 128), F32),
            pltpu.VMEM((NLON, 2, 8, 128), F32),
            pltpu.VMEM((NLAT, 2, 16, 128), F32),
            pltpu.VMEM((NLAT, 2, 16, 128), F32),
            pltpu.VMEM((3, 64, 128), F32),
            pltpu.VMEM((256, 512), F32),
            pltpu.VMEM((2, 256, 512), BF16),
            pltpu.VMEM((256 * 8, TLON), F32),
            pltpu.VMEM((8, 256), F32),
            pltpu.VMEM((2, 64, 8, 256), F32),
            pltpu.VMEM((4, MEM, TLON), F32),
            pltpu.VMEM(tile, F32),
            pltpu.SemaphoreType.DMA((12,)),
            pltpu.SemaphoreType.DMA((GROUPS + 1,)),
            pltpu.SemaphoreType.DMA((COPIES,)),
            pltpu.SemaphoreType.DMA((COPIES,)),
        ],
        compiler_params=pltpu.CompilerParams(
            collective_id=0, has_side_effects=True, vmem_limit_bytes=60 * 1024 * 1024
        ),
    )(
        ce, cn, cells.reshape(8, 128), misfit.reshape(FIELDS, 8, 128), kern, ens,
        psrc.reshape(8, 128), pdst.reshape(8, 128), taper.reshape(8, 128), var,
    )
    return pl.pallas_call(
        hand_over,
        out_shape=(
            jax.ShapeDtypeStruct((LEV,) + tile, F32),
            jax.ShapeDtypeStruct(tile, F32),
        ),
        in_specs=[hbm] * 2,
        out_specs=(hbm, hbm),
        scratch_shapes=[
            pltpu.VMEM((LEV,) + tile, F32),
            pltpu.VMEM(tile, F32),
            pltpu.SemaphoreType.DMA((PIECES + 1,)),
            pltpu.SemaphoreType.DMA((PIECES + 1,)),
        ],
        compiler_params=pltpu.CompilerParams(vmem_limit_bytes=60 * 1024 * 1024),
    )(field, prior)


def solution(mesh):
    in_specs = (
        P(None, "lat", "lon"),
        P(None, "lat", "lon"),
        P("lat", "lon", None),
        P(None, "lat", "lon", None),
        P(),
        P(None, "lat", "lon"),
        P(("lon", "lat")),
        P(("lon", "lat")),
        P(("lon", "lat")),
        P("lat", "lon"),
    )
    out_specs = (P(None, "lat", "lon"), P("lat", "lon"))
    return jax.shard_map(
        per_device, mesh=mesh, in_specs=in_specs, out_specs=out_specs, check_vma=False
    )
```

```python
import jax
import jax.numpy as jnp
from jax import lax
from jax.experimental import pallas as pl
from jax.experimental.pallas import tpu as pltpu
from jax.sharding import PartitionSpec as P

MESH = pl.DeviceIdType.MESH
F32, BF16, I32, I16 = jnp.float32, jnp.bfloat16, jnp.int32, jnp.int16

TLAT, TLON, LEV, BLK, MEM = 64, 128, 72, 16, 64
NLON, NLAT = 16, 8
FIELDS = 5
EXT = 7
ROWS = TLAT + 16
GROUPS = 3
PIECES = 8
KG = LEV // GROUPS
LEVELS = KG
ROUNDS = 3
CHUNKS = 8
COPIES = 8 + 2 + 4 * ROUNDS * GROUPS + 15 + 7 + 15 + 1 + 3 + 3


def iota(shape, dim):
    return lax.broadcasted_iota(I32, shape, dim)


def dot_nt(a, b):
    return lax.dot_general(a, b, (((1,), (1,)), ((), ())), preferred_element_type=F32)


def dot_tn(a, b):
    return lax.dot_general(a, b, (((0,), (0,)), ((), ())), preferred_element_type=F32)


def dot_nn(a, b):
    return lax.dot_general(a, b, (((1,), (0,)), ((), ())), preferred_element_type=F32)


def spread_row(row, dtype, rows):
    few = jnp.broadcast_to(row, (16, 128)).astype(dtype)
    return jnp.concatenate([few] * (rows // 16), axis=0)


def select(mask, row, rows):
    return jnp.where(mask, spread_row(row, BF16, rows), jnp.zeros((), BF16))


def one_hot(mask):
    return jnp.where(mask, jnp.ones((), BF16), jnp.zeros((), BF16))


def parts_of(x, count):
    parts = []
    for _ in range(count):
        part = x.astype(BF16)
        parts.append(part)
        x = x - part.astype(F32)
    return parts


def kernel(
    ce_hbm, cn_hbm, cells_hbm, misfit_hbm, kern_hbm, ens_hbm, psrc_hbm, pdst_hbm, taper_hbm, var_hbm,
    out_hbm, prior_hbm,
    cells, misfit, kern, psrc, pdst, taper, var_ref,
    ce, cn, aw, asn, c0, field, field16, last, ens, area, halo_e, halo_w, pack_e, pack_w,
    cpack, chalo, crow, crhalo, shifted,
    fpack, fhalo_e, fhalo_w, move, ends, every, to_first, frow_n, frow_s, frhalo_n, frhalo_s,
    slots1, route1, slots2, route2, keys, weights, weights16,
    partial, own, table, ycol, prior,
    local_sem, out_sem, send_sem, recv_sem,
):
    lon, lat = lax.axis_index("lon"), lax.axis_index("lat")
    core, x, y_lo = lon % 2, (lon // 2) % 4, lon // 8
    z, y_hi = lat // 2, lat % 2
    y = y_hi * 2 + y_lo

    def shift_lon(s):
        return (lon + s + NLON) % NLON

    def shift_lat(s):
        return (lat + s + NLAT) % NLAT

    def device(xx, yy, zz, cc):
        return {"lon": (yy % 2) * 8 + xx * 2 + cc, "lat": zz * 2 + yy // 2}

    rest = pl.ds(1, LEV - 1)
    first_axis, second_axis, third_axis = (1 - core, core, 0), (0, 1 - core, core), (core, 0, 1 - core)

    def plane_peer(i, j):
        place = [(v + i * a + j * b) % 4 for v, a, b in zip((x, y, z), first_axis, second_axis)]
        return device(*place, core)

    def line_peer(i):
        return device(*[(v + i * a) % 4 for v, a in zip((x, y, z), third_axis)], core)

    ce_in = pltpu.make_async_copy(ce_hbm.at[rest], ce.at[rest], local_sem.at[0])
    cn_in = pltpu.make_async_copy(cn_hbm.at[rest], cn.at[rest, pl.ds(8, TLAT), :], local_sem.at[1])
    ens_in = pltpu.make_async_copy(ens_hbm, ens, local_sem.at[2])
    small = [
        pltpu.make_async_copy(src, dst, local_sem.at[3 + n])
        for n, (src, dst) in enumerate((
            (cells_hbm, cells), (misfit_hbm, misfit), (kern_hbm, kern), (psrc_hbm, psrc),
            (pdst_hbm, pdst), (taper_hbm, taper), (var_hbm, var_ref),
            (ce_hbm.at[0], ce.at[0]), (cn_hbm.at[0], cn.at[0, pl.ds(8, TLAT), :]),
        ))
    ]
    for copy in small + [ce_in]:
        copy.start()

    barrier = pltpu.get_barrier_semaphore()
    peers = [{"lon": shift_lon(i), "lat": lat} for i in range(1, NLON)]
    peers += [{"lon": lon, "lat": shift_lat(i)} for i in range(1, NLAT)]
    peers += [plane_peer(i, j) for i in range(4) for j in range(4) if i or j]
    peers += [{"lon": shift_lon(i), "lat": shift_lat(j)} for i in (-1, 1) for j in (-1, 1)]
    for peer in peers:
        pl.semaphore_signal(barrier, inc=1, device_id=peer, device_id_type=MESH)

    used = [0]

    def remote(src, dst, peer):
        n = used[0]
        used[0] += 1
        return pltpu.make_async_remote_copy(
            src_ref=src, dst_ref=dst, send_sem=send_sem.at[n], recv_sem=recv_sem.at[n],
            device_id=peer, device_id_type=MESH,
        )

    lane = iota((TLAT, TLON), 1)
    lane32 = lane % 32

    row, col = iota((256, 256), 0), iota((256, 256), 1)
    shift = (row < 128) & (((col < 128) & (row == col + 1)) | ((col >= 128) & (row + 129 == col)))
    edge = ((row >= 160) & (row < 192) & (col == 127)) | ((row >= 128) & (row < 160) & (col == 128))
    move[...] = jnp.where(shift | edge, 1.0, 0.0).astype(BF16)
    end = ((row % 128 == 127) & (col % 128 < 32)) | ((row % 128 == 0) & (col % 128 >= 32) & (col % 128 < 64))
    end = end & (row // 128 == col // 128)
    ends[...] = jnp.where(end, 1.0, 0.0).astype(BF16)
    row, col = iota((128, 128), 0), iota((128, 128), 1)
    every[...] = jnp.where(row == 127, 1.0, 0.0).astype(BF16)
    to_first[...] = jnp.where(col == 0, 1.0, 0.0).astype(BF16)

    for copy in small:
        copy.wait()
    cn_in.start()

    columns = [jnp.zeros((TLAT, TLON), F32) for _ in range(FIELDS)]
    cell_row, cell_col = cells[...] >> 7, cells[...] & 127
    number = iota((128, 128), 0).astype(I16)
    for q in range(CHUNKS):
        in_row = number[:TLAT] == spread_row(cell_row[q : q + 1], I16, TLAT)
        in_col = one_hot(number == spread_row(cell_col[q : q + 1], I16, TLON))
        weighted = []
        for t in range(FIELDS):
            for part in parts_of(misfit[t, q : q + 1, :], 2):
                weighted.append(select(in_row, part.astype(F32), TLAT))
        placed = dot_nt(jnp.concatenate(weighted, axis=0), in_col)
        for t in range(FIELDS):
            base = 2 * t * TLAT
            columns[t] += placed[base : base + TLAT] + placed[base + TLAT : base + 2 * TLAT]
    for t in range(FIELDS):
        area[t, 8 : 8 + TLAT, :] = columns[t]

    ens_in.start()

    area[5, 8 : 8 + TLAT, :] = ce[0]
    area[6, 8 : 8 + TLAT, :] = cn[0, 8 : 8 + TLAT, :]
    first = jnp.zeros((TLAT, TLON), F32)
    final = jnp.zeros((TLAT, TLON), F32)
    for n in range(EXT):
        value = area[n, 8 : 8 + TLAT, :]
        here = (lane >= 4 * n) & (lane < 4 * n + 4)
        first = jnp.where(here, pltpu.roll(value, 4 * n, 1) if n else value, first)
        final = jnp.where(here, pltpu.roll(value, 4 * n + 4, 1), final)
    pack_w[...] = first
    pack_e[...] = final

    pl.semaphore_wait(barrier, len(peers))

    east = {"lon": shift_lon(1), "lat": lat}
    west = {"lon": shift_lon(-1), "lat": lat}
    north = {"lon": lon, "lat": shift_lat(1)}
    south = {"lon": lon, "lat": shift_lat(-1)}
    mid, low8, high8 = pl.ds(8, TLAT), pl.ds(0, 8), pl.ds(TLAT + 8, 8)
    edges = [
        remote(area.at[:, pl.ds(TLAT, 8), :], area.at[:, low8, :], north),
        remote(area.at[:, pl.ds(8, 8), :], area.at[:, high8, :], south),
        remote(pack_e, halo_w.at[mid, :], east),
        remote(pack_w, halo_e.at[mid, :], west),
        remote(pack_e.at[pl.ds(TLAT - 8, 8), :], halo_w.at[low8, :], {"lon": shift_lon(1), "lat": shift_lat(1)}),
        remote(pack_e.at[pl.ds(0, 8), :], halo_w.at[high8, :], {"lon": shift_lon(1), "lat": shift_lat(-1)}),
        remote(pack_w.at[pl.ds(TLAT - 8, 8), :], halo_e.at[low8, :], {"lon": shift_lon(-1), "lat": shift_lat(1)}),
        remote(pack_w.at[pl.ds(0, 8), :], halo_e.at[high8, :], {"lon": shift_lon(-1), "lat": shift_lat(-1)}),
    ]
    for copy in edges:
        copy.start()

    ce_in.wait()

    def pack_courant(kb, acc):
        faces = [ce[kb * 8 + i].astype(BF16) for i in range(8)]
        tips = dot_nn(jnp.concatenate(faces, axis=0), every[...])
        for i in range(8):
            acc = jnp.where(lane == kb * 8 + i, tips[i * TLAT : (i + 1) * TLAT], acc)
        return acc

    cpack[...] = lax.fori_loop(0, LEV // 8, pack_courant, jnp.zeros((TLAT, TLON), F32))
    cn_in.wait()
    cn_rows = cn.reshape(LEV * (TLAT + 8), TLON)
    last_row = cn_rows[pl.ds(TLAT + 7, LEV, stride=TLAT + 8), :] * jnp.where(lat < NLAT - 1, 1.0, 0.0)
    crow[...] = last_row
    cn_rows[pl.ds(TLAT + 7, LEV, stride=TLAT + 8), :] = last_row
    courants = [remote(crow, crhalo, north), remote(cpack, chalo, east)]
    for copy in courants:
        copy.start()

    total = jnp.zeros((128, 128), F32)
    slot1 = jnp.zeros((128, 128), F32)
    slot2 = jnp.zeros((128, 128), F32)
    before = jnp.where(iota((128, 128), 0) < iota((128, 128), 1), 1.0, 0.0).astype(BF16)
    ones = jnp.ones((128, 128), BF16)
    src, dst = psrc[...], pdst[...]
    s_lon, s_lat = src >> 8, (src >> 5) & 7
    s_x, s_y, s_z = (s_lon >> 1) & 3, (s_lat & 1) * 2 + (s_lon >> 3), s_lat >> 1
    s_slot = jnp.where((s_lon & 1) == 0, s_z * 16 + s_y * 4 + s_x, s_x * 16 + s_z * 4 + s_y)
    key1 = ((s_lon & 1) * 128 + ((src >> 3) & 3) * 32 + (dst & 31)).astype(F32)
    key2_high, key2_low = (s_slot * 8).astype(F32), (src & 7).astype(F32)
    tile = dst >> 5
    for q in range(CHUNKS):
        at = slice(q, q + 1)
        here = iota((128, 128), 0) == tile[at]
        mine = number == spread_row(tile[at], I16, 128)
        mark = one_hot(mine)
        count = dot_nn(mark, before) + total
        total += dot_nn(mark, ones)
        rank = jnp.sum(jnp.where(here, count, 0.0), axis=0, keepdims=True).astype(I32)
        at_low = one_hot(number == spread_row(rank, I16, 128))
        at_high = one_hot(number == spread_row(rank + 64, I16, 128))
        slot1 += dot_nt(select(mine, key1[at], 128), at_low)
        slot1 += dot_nt(select(mine, key2_high[at], 128), at_high)
        slot1 += dot_nt(select(mine, key2_low[at], 128), at_high)
        slot2 += dot_nt(select(mine, taper[at, :], 128), at_low)
    for d in range(NLON):
        slots1[d, 0] = slot1[d * 8 : d * 8 + 8]
        slots1[d, 1] = slot2[d * 8 : d * 8 + 8]

    routes = [
        remote(slots1.at[shift_lon(i)], route1.at[lon], {"lon": shift_lon(i), "lat": lat})
        for i in range(1, NLON)
    ]
    for copy in routes:
        copy.start()

    for copy in edges[:4]:
        copy.wait_recv()
    base = area[0, 8 : 8 + TLAT, :]
    shifted[0] = base
    shifted[1] = jnp.where(lane == 127, pltpu.roll(halo_e[8 : 8 + TLAT, :], 127, 1), pltpu.roll(base, 127, 1))
    shifted[2] = jnp.where(lane == 0, pltpu.roll(halo_w[8 : 8 + TLAT, :], 125, 1), pltpu.roll(base, 1, 1))
    shifted[3] = area[0, 9 : 9 + TLAT, :]
    shifted[4] = area[0, 7 : 7 + TLAT, :]

    for copy in courants:
        copy.wait_recv()
    cn_rows[pl.ds(7, LEV, stride=TLAT + 8), :] = crhalo[...] * jnp.where(lat > 0, 1.0, 0.0)
    field_rows = field.reshape(LEV * ROWS, TLON)

    def block(t, g, halo, kb, pack):
        base = g * KG + kb * LEVELS
        if t > 1:
            rows = []
            for i in range(LEVELS):
                mine = jnp.where(lane32 == kb * LEVELS + i, halo, 0.0).astype(BF16)
                rows.append(jnp.concatenate([field16[base + i], mine], axis=1))
            moved = dot_nn(jnp.concatenate(rows, axis=0), move[...])
        else:
            rows = [jnp.where(lane == base + i, halo, 0.0).astype(BF16) for i in range(LEVELS)]
            moved = dot_nn(jnp.concatenate(rows, axis=0), to_first[...])
        rounded = []
        for i in range(LEVELS):
            k = base + i
            kk = kern[k]
            if t == 1:
                faces = ce[k]
                pe = jnp.maximum(faces, 0.0)
                behind = jnp.where(lane == 0, moved[i * TLAT : (i + 1) * TLAT], pltpu.roll(faces, 1, 1))
                w = jnp.minimum(behind, 0.0)
                pn = jnp.maximum(cn[k, 8 : 8 + TLAT, :], 0.0)
                s = jnp.minimum(cn[k, 7 : 7 + TLAT, :], 0.0)
                c = (1.0 - pe) + w - pn + s
                ce[k] = pe
                cn[k, 8 : 8 + TLAT, :] = pn
                aw[k], asn[k], c0[k] = w, s, c
                new = kk * (
                    c * shifted[0] + pe * shifted[1] - w * shifted[2] + pn * shifted[3] - s * shifted[4]
                    + area[1, 8 : 8 + TLAT, :]
                )
            else:
                level_rows = slice(i * TLAT, (i + 1) * TLAT)
                new = (
                    c0[k] * field[k, 8 : 8 + TLAT, :]
                    + ce[k] * moved[level_rows, :TLON] - aw[k] * moved[level_rows, TLON:]
                    + cn[k, 8 : 8 + TLAT, :] * field[k, 9 : 9 + TLAT, :]
                    - asn[k] * field[k, 7 : 7 + TLAT, :] + kk * area[t, 8 : 8 + TLAT, :]
                )
            if t == 4:
                last[k] = new
                continue
            field[k, 8 : 8 + TLAT, :] = new
            new16 = new.astype(BF16)
            field16[k] = new16
            rounded.append(new16)
        if t == 4:
            return pack
        pairs = [jnp.concatenate(rounded[i : i + 2], axis=1) for i in range(0, LEVELS, 2)]
        tips = dot_nn(jnp.concatenate(pairs, axis=0), ends[...])
        for i in range(LEVELS):
            tip = tips[i // 2 * TLAT : (i // 2 + 1) * TLAT, i % 2 * TLON : (i % 2 + 1) * TLON]
            pack = jnp.where(lane32 == kb * LEVELS + i, tip, pack)
        return pack

    sent = {}
    outs = []

    def run_group(t, g, share=None):
        start = g * KG * ROWS
        halo = chalo[...]
        if t > 1:
            for copy in sent[t - 1, g]:
                copy.wait_recv()
            field_rows[pl.ds(start + 7, KG, stride=ROWS), :] = frhalo_s[t - 2, g]
            field_rows[pl.ds(start + 8 + TLAT, KG, stride=ROWS), :] = frhalo_n[t - 2, g]
            halo = jnp.where(lane < 32, fhalo_w[t - 2, g], fhalo_e[t - 2, g])
        if share is not None:
            add_weights(share, 0)
        pack = block(t, g, halo, 0, jnp.zeros((TLAT, TLON), F32))
        if t == 4:
            levels = pl.ds(g * KG, KG)
            outs.append(pltpu.make_async_copy(last.at[levels], out_hbm.at[levels], out_sem.at[g]))
            outs[-1].start()
            return
        fpack[t - 1, g] = pack
        frow_n[t - 1, g] = field_rows[pl.ds(start + 7 + TLAT, KG, stride=ROWS), :]
        frow_s[t - 1, g] = field_rows[pl.ds(start + 8, KG, stride=ROWS), :]
        sent[t, g] = [
            remote(frow_n.at[t - 1, g], frhalo_s.at[t - 1, g], north),
            remote(frow_s.at[t - 1, g], frhalo_n.at[t - 1, g], south),
            remote(fpack.at[t - 1, g], fhalo_w.at[t - 1, g], east),
            remote(fpack.at[t - 1, g], fhalo_e.at[t - 1, g], west),
        ]
        for copy in sent[t, g]:
            copy.start()

    run_group(1, 0)
    run_group(1, 1)
    run_group(1, 2)

    route1[lon] = slots1[lon]
    for copy in routes:
        copy.wait_recv()
    for n in range(2):
        for a in range(NLAT):
            slots2[a, n] = jnp.concatenate([route1[d, n, a : a + 1, :] for d in range(NLON)], axis=0)
    routes2 = [
        remote(slots2.at[shift_lat(i)], route2.at[lat], {"lon": lon, "lat": shift_lat(i)})
        for i in range(1, NLAT)
    ]
    for copy in routes2:
        copy.start()
    route2[lat] = slots2[lat]

    for copy in edges[4:]:
        copy.wait_recv()

    wide_lane = iota((ROWS, TLON), 1)

    def widened(n):
        from_east = halo_e[...] if n == 0 else pltpu.roll(halo_e[...], 128 - 4 * n, 1)
        from_west = pltpu.roll(halo_w[...], 124 - 4 * n, 1)
        side = jnp.where(wide_lane < 64, from_east, from_west)
        return jnp.concatenate([area[n], side], axis=1)

    def up(v, axis):
        return pltpu.roll(v, v.shape[axis] - 1, axis)

    def down(v, axis):
        return pltpu.roll(v, 1, axis)

    forced = [widened(t) for t in range(FIELDS)]
    east0 = widened(5)
    global_row = lat * TLAT - 8 + iota((ROWS, 2 * TLON), 0)
    inside = (global_row >= 0) & (global_row < NLAT * TLAT - 1)
    north0 = jnp.where(inside, widened(6), 0.0)
    pe0, pn0 = jnp.maximum(east0, 0.0), jnp.maximum(north0, 0.0)
    aw0, as0 = -jnp.minimum(down(east0, 1), 0.0), -jnp.minimum(down(north0, 0), 0.0)
    c00 = 1.0 - pe0 - aw0 - pn0 - as0
    k0 = kern[0]
    level = k0 * forced[0]
    surface_wide = level
    for t in range(1, FIELDS):
        level = (
            c00 * level + pe0 * up(level, 1) + aw0 * down(level, 1)
            + pn0 * up(level, 0) + as0 * down(level, 0) + k0 * forced[t]
        )
        surface_wide = surface_wide + level
    surface = surface_wide[8 : 8 + TLAT, :TLON]
    prior[...] = surface

    ens_in.wait()
    rounded = surface.astype(BF16).astype(F32)

    @pl.loop(0, MEM)
    def _(m):
        product = ens[m].astype(F32) * rounded
        for r in range(4):
            at = pl.multiple_of((r * MEM + m) * 8, 8)
            partial[pl.ds(at, 8), :] = product[r * 16 : r * 16 + 8] + product[r * 16 + 8 : r * 16 + 16]

    row_sums = partial[pl.ds(0, 256, stride=8), :]
    for s in range(1, 8):
        row_sums += partial[pl.ds(s, 256, stride=8), :]
    in_block = jnp.where(iota((8, TLON), 0) == iota((8, TLON), 1) // BLK, 1.0, 0.0).astype(BF16)
    own[...] = sum(dot_nt(in_block, part) for part in parts_of(row_sums, 3))

    slot = jnp.where(core == 0, z * 16 + y * 4 + x, x * 16 + z * 4 + y)
    sibling = device(x, y, z, 1 - core)
    group = pl.ds(slot // 16 * 16, 16)
    plane = [
        remote(own, table.at[core, slot], plane_peer(i, j))
        for i in (2, 1, 3, 0) for j in (2, 1, 3, 0) if i or j
    ]
    for copy in plane:
        copy.start()
    table[core, slot] = own[...]
    shares, line = [], []

    def gather_line():
        for copy in plane:
            copy.wait_recv()
        line.extend(remote(table.at[core, group], table.at[core, group], line_peer(i)) for i in (2, 1, 3))
        shares.append(remote(table.at[core, group], table.at[core, group], sibling))
        for copy in line + shares:
            copy.start()

    def share_line():
        for n, i in enumerate((1, 3, 2)):
            line[(1, 2, 0)[n]].wait_recv()
            rows = pl.ds((slot // 16 + (4 - i)) % 4 * 16, 16)
            copy = remote(table.at[core, rows], table.at[core, rows], sibling)
            copy.start()
            shares.append(copy)

    run_group(2, 0)
    run_group(2, 1)
    run_group(2, 2)

    gather_line()

    for copy in routes2:
        copy.wait_recv()
    half = iota((16, 128), 1) < 64
    for a in range(4):
        one, two = route2[a, 0], route2[a + 4, 0]
        at = slice(a * 16, a * 16 + 16)
        keys[0, at] = jnp.where(half, one, pltpu.roll(two, 64, 1))
        keys[1, at] = jnp.where(half, pltpu.roll(one, 64, 1), two)
        keys[2, at] = jnp.where(half, route2[a, 1], pltpu.roll(route2[a + 4, 1], 64, 1))
    weights[...] = jnp.zeros_like(weights)

    def add_weights(i, carry):
        at = pl.ds(i * 8 if isinstance(i, int) else pl.multiple_of(i * 8, 8), 8)
        key1, key2, weight = keys[0, at, :].astype(I32), keys[1, at, :].astype(I32), keys[2, at, :]
        number = iota((128, 128), 0).astype(I16)
        lhs, rhs = [], []
        for u in range(8):
            one = slice(u, u + 1)
            match = [number == spread_row(key1[one] - r, I16, 128) for r in (0, 128)]
            lhs.append(jnp.concatenate([select(m, weight[one], 128) for m in match], axis=0))
            match = [number == spread_row(key2[one] - r, I16, 128) for r in (0, 128, 256, 384)]
            rhs.append(jnp.concatenate([one_hot(m) for m in match], axis=0))
        weights[...] += dot_nt(jnp.concatenate(lhs, axis=1), jnp.concatenate(rhs, axis=1))
        return carry

    lax.fori_loop(0, 2, add_weights, 0)

    run_group(3, 0, 2)
    run_group(3, 1, 3)
    run_group(3, 2, 4)

    run_group(4, 0, 5)
    share_line()
    run_group(4, 1, 6)
    run_group(4, 2, 7)

    w_parts = parts_of(weights[...], 2)
    weights16[0] = w_parts[0]
    weights16[1] = w_parts[1]

    for copy in shares:
        copy.wait_recv()
    combined4 = jnp.zeros((128, 256), F32)
    for q in range(4):
        table_part = table[q // 2, (q % 2) * 32 : (q % 2) * 32 + 32].reshape(256, 256)
        t_high, t_low = parts_of(table_part, 2)
        w_rows, w_cols = slice(q // 2 * 128, q // 2 * 128 + 128), slice(q % 2 * 256, q % 2 * 256 + 256)
        w_high, w_low = weights16[0, w_rows, w_cols], weights16[1, w_rows, w_cols]
        combined4 += dot_nn(w_high, t_high) + dot_nn(w_high, t_low) + dot_nn(w_low, t_high)
    combined = combined4[:32, :64]
    for r in range(1, 4):
        combined += combined4[r * 32 : (r + 1) * 32, r * 64 : (r + 1) * 64]
    for r in range(4):
        ycol[r] = dot_tn(combined[r * 8 : r * 8 + 8].astype(BF16), in_block)

    def add_member(m, acc):
        rows = [jnp.broadcast_to(ycol[r, pl.ds(m, 1), :], (BLK, TLON)) for r in range(4)]
        return acc + ens[m].astype(F32) * jnp.concatenate(rows, axis=0)

    prior[...] = lax.fori_loop(0, MEM, add_member, var_ref[...] * prior[...], unroll=8)
    outs.append(pltpu.make_async_copy(prior, prior_hbm, out_sem.at[GROUPS]))
    outs[-1].start()

    for copy in outs:
        copy.wait()
    flights = edges + courants + routes + routes2 + plane + line + shares
    flights += [copy for group in sent.values() for copy in group]
    for copy in flights:
        copy.wait_send()


def hand_over(field, prior, field_out, prior_out, field_held, prior_held, in_sem, out_sem):
    steps = LEV // PIECES
    parts = [(prior, prior_held, prior_out)]
    for n in range(PIECES):
        levels = pl.ds(n * steps, steps)
        parts.append((field.at[levels], field_held.at[levels], field_out.at[levels]))
    loads = [
        pltpu.make_async_copy(src, held, in_sem.at[n]) for n, (src, held, _) in enumerate(parts)
    ]
    stores = [
        pltpu.make_async_copy(held, dst, out_sem.at[n]) for n, (_, held, dst) in enumerate(parts)
    ]
    for load in loads:
        load.start()
    for load, store in zip(loads, stores):
        load.wait()
        store.start()
    for store in stores:
        store.wait()


def per_device(ce, cn, cells, misfit, kern, ens, psrc, pdst, taper, var):
    hbm = pl.BlockSpec(memory_space=pl.ANY)
    tile = (TLAT, TLON)
    field, prior = pl.pallas_call(
        kernel,
        out_shape=(
            jax.ShapeDtypeStruct((LEV,) + tile, F32),
            jax.ShapeDtypeStruct(tile, F32),
        ),
        in_specs=[hbm] * 10,
        out_specs=(hbm, hbm),
        scratch_shapes=[
            pltpu.VMEM((8, 128), I32),
            pltpu.VMEM((FIELDS, 8, 128), F32),
            pltpu.SMEM((LEV,), F32),
            pltpu.VMEM((8, 128), I32),
            pltpu.VMEM((8, 128), I32),
            pltpu.VMEM((8, 128), F32),
            pltpu.VMEM(tile, F32),
            pltpu.VMEM((LEV,) + tile, F32),
            pltpu.VMEM((LEV, TLAT + 8, TLON), F32),
            pltpu.VMEM((LEV,) + tile, F32),
            pltpu.VMEM((LEV,) + tile, F32),
            pltpu.VMEM((LEV,) + tile, F32),
            pltpu.VMEM((LEV, ROWS, TLON), F32),
            pltpu.VMEM((LEV,) + tile, BF16),
            pltpu.VMEM((LEV,) + tile, F32),
            pltpu.VMEM((MEM,) + tile, BF16),
            pltpu.VMEM((EXT, ROWS, TLON), F32),
            pltpu.VMEM((ROWS, TLON), F32),
            pltpu.VMEM((ROWS, TLON), F32),
            pltpu.VMEM(tile, F32),
            pltpu.VMEM(tile, F32),
            pltpu.VMEM(tile, F32),
            pltpu.VMEM(tile, F32),
            pltpu.VMEM((LEV, TLON), F32),
            pltpu.VMEM((LEV, TLON), F32),
            pltpu.VMEM((5,) + tile, F32),
        ]
        + [pltpu.VMEM((ROUNDS, GROUPS) + tile, F32) for _ in range(3)]
        + [pltpu.VMEM((256, 256), BF16) for _ in range(2)]
        + [pltpu.VMEM((128, 128), BF16) for _ in range(2)]
        + [pltpu.VMEM((ROUNDS, GROUPS, KG, TLON), F32) for _ in range(4)]
        + [
            pltpu.VMEM((NLON, 2, 8, 128), F32),
            pltpu.VMEM((NLON, 2, 8, 128), F32),
            pltpu.VMEM((NLAT, 2, 16, 128), F32),
            pltpu.VMEM((NLAT, 2, 16, 128), F32),
            pltpu.VMEM((3, 64, 128), F32),
            pltpu.VMEM((256, 512), F32),
            pltpu.VMEM((2, 256, 512), BF16),
            pltpu.VMEM((256 * 8, TLON), F32),
            pltpu.VMEM((8, 256), F32),
            pltpu.VMEM((2, 64, 8, 256), F32),
            pltpu.VMEM((4, MEM, TLON), F32),
            pltpu.VMEM(tile, F32),
            pltpu.SemaphoreType.DMA((12,)),
            pltpu.SemaphoreType.DMA((GROUPS + 1,)),
            pltpu.SemaphoreType.DMA((COPIES,)),
            pltpu.SemaphoreType.DMA((COPIES,)),
        ],
        compiler_params=pltpu.CompilerParams(
            collective_id=0, has_side_effects=True, vmem_limit_bytes=60 * 1024 * 1024
        ),
    )(
        ce, cn, cells.reshape(8, 128), misfit.reshape(FIELDS, 8, 128), kern, ens,
        psrc.reshape(8, 128), pdst.reshape(8, 128), taper.reshape(8, 128), var,
    )
    return pl.pallas_call(
        hand_over,
        out_shape=(
            jax.ShapeDtypeStruct((LEV,) + tile, F32),
            jax.ShapeDtypeStruct(tile, F32),
        ),
        in_specs=[hbm] * 2,
        out_specs=(hbm, hbm),
        scratch_shapes=[
            pltpu.VMEM((LEV,) + tile, F32),
            pltpu.VMEM(tile, F32),
            pltpu.SemaphoreType.DMA((PIECES + 1,)),
            pltpu.SemaphoreType.DMA((PIECES + 1,)),
        ],
        compiler_params=pltpu.CompilerParams(vmem_limit_bytes=60 * 1024 * 1024),
    )(field, prior)


def solution(mesh):
    in_specs = (
        P(None, "lat", "lon"),
        P(None, "lat", "lon"),
        P("lat", "lon", None),
        P(None, "lat", "lon", None),
        P(),
        P(None, "lat", "lon"),
        P(("lon", "lat")),
        P(("lon", "lat")),
        P(("lon", "lat")),
        P("lat", "lon"),
    )
    out_specs = (P(None, "lat", "lon"), P("lat", "lon"))
    return jax.shard_map(
        per_device, mesh=mesh, in_specs=in_specs, out_specs=out_specs, check_vma=False
    )
```

```python
import jax
import jax.numpy as jnp
from jax import lax
from jax.experimental import pallas as pl
from jax.experimental.pallas import tpu as pltpu
from jax.sharding import PartitionSpec as P

MESH = pl.DeviceIdType.MESH
F32, BF16, I32, I16 = jnp.float32, jnp.bfloat16, jnp.int32, jnp.int16

TLAT, TLON, LEV, BLK, MEM = 64, 128, 72, 16, 64
NLON, NLAT = 16, 8
FIELDS = 5
EXT = 7
ROWS = TLAT + 16
GROUPS = 3
PIECES = 8
KG = LEV // GROUPS
LEVELS = KG
ROUNDS = 3
CHUNKS = 8
COPIES = 8 + 2 + 4 * ROUNDS * GROUPS + 15 + 7 + 15 + 1 + 3 + 3


def iota(shape, dim):
    return lax.broadcasted_iota(I32, shape, dim)


def dot_nt(a, b):
    return lax.dot_general(a, b, (((1,), (1,)), ((), ())), preferred_element_type=F32)


def dot_tn(a, b):
    return lax.dot_general(a, b, (((0,), (0,)), ((), ())), preferred_element_type=F32)


def dot_nn(a, b):
    return lax.dot_general(a, b, (((1,), (0,)), ((), ())), preferred_element_type=F32)


def spread_row(row, dtype, rows):
    few = jnp.broadcast_to(row, (16, 128)).astype(dtype)
    return jnp.concatenate([few] * (rows // 16), axis=0)


def select(mask, row, rows):
    return jnp.where(mask, spread_row(row, BF16, rows), jnp.zeros((), BF16))


def one_hot(mask):
    return jnp.where(mask, jnp.ones((), BF16), jnp.zeros((), BF16))


def parts_of(x, count):
    parts = []
    for _ in range(count):
        part = x.astype(BF16)
        parts.append(part)
        x = x - part.astype(F32)
    return parts


def kernel(
    ce_hbm, cn_hbm, cells_hbm, misfit_hbm, kern_hbm, ens_hbm, psrc_hbm, pdst_hbm, taper_hbm, var_hbm,
    out_hbm, prior_hbm,
    cells, misfit, kern, psrc, pdst, taper, var_ref,
    ce, cn, aw, asn, c0, field, field16, last, ens, area, halo_e, halo_w, pack_e, pack_w,
    cpack, chalo, crow, crhalo, shifted,
    fpack, fhalo_e, fhalo_w, move, ends, every, to_first, frow_n, frow_s, frhalo_n, frhalo_s,
    slots1, route1, slots2, route2, keys, weights, weights16,
    partial, own, table, ycol, prior,
    local_sem, out_sem, send_sem, recv_sem,
):
    lon, lat = lax.axis_index("lon"), lax.axis_index("lat")
    core, x, y_lo = lon % 2, (lon // 2) % 4, lon // 8
    z, y_hi = lat // 2, lat % 2
    y = y_hi * 2 + y_lo

    def shift_lon(s):
        return (lon + s + NLON) % NLON

    def shift_lat(s):
        return (lat + s + NLAT) % NLAT

    def device(xx, yy, zz, cc):
        return {"lon": (yy % 2) * 8 + xx * 2 + cc, "lat": zz * 2 + yy // 2}

    rest = pl.ds(1, LEV - 1)
    first_axis, second_axis, third_axis = (1 - core, core, 0), (0, 1 - core, core), (core, 0, 1 - core)

    def plane_peer(i, j):
        place = [(v + i * a + j * b) % 4 for v, a, b in zip((x, y, z), first_axis, second_axis)]
        return device(*place, core)

    def line_peer(i):
        return device(*[(v + i * a) % 4 for v, a in zip((x, y, z), third_axis)], core)

    ce_in = pltpu.make_async_copy(ce_hbm.at[rest], ce.at[rest], local_sem.at[0])
    cn_in = pltpu.make_async_copy(cn_hbm.at[rest], cn.at[rest, pl.ds(8, TLAT), :], local_sem.at[1])
    ens_in = pltpu.make_async_copy(ens_hbm, ens, local_sem.at[2])
    small = [
        pltpu.make_async_copy(src, dst, local_sem.at[3 + n])
        for n, (src, dst) in enumerate((
            (cells_hbm, cells), (misfit_hbm, misfit), (kern_hbm, kern), (psrc_hbm, psrc),
            (pdst_hbm, pdst), (taper_hbm, taper), (var_hbm, var_ref),
            (ce_hbm.at[0], ce.at[0]), (cn_hbm.at[0], cn.at[0, pl.ds(8, TLAT), :]),
        ))
    ]
    for copy in small + [ce_in]:
        copy.start()

    barrier = pltpu.get_barrier_semaphore()
    peers = [{"lon": shift_lon(i), "lat": lat} for i in range(1, NLON)]
    peers += [{"lon": lon, "lat": shift_lat(i)} for i in range(1, NLAT)]
    peers += [plane_peer(i, j) for i in range(4) for j in range(4) if i or j]
    peers += [{"lon": shift_lon(i), "lat": shift_lat(j)} for i in (-1, 1) for j in (-1, 1)]
    for peer in peers:
        pl.semaphore_signal(barrier, inc=1, device_id=peer, device_id_type=MESH)

    used = [0]

    def remote(src, dst, peer):
        n = used[0]
        used[0] += 1
        return pltpu.make_async_remote_copy(
            src_ref=src, dst_ref=dst, send_sem=send_sem.at[n], recv_sem=recv_sem.at[n],
            device_id=peer, device_id_type=MESH,
        )

    lane = iota((TLAT, TLON), 1)
    lane32 = lane % 32

    row, col = iota((256, 256), 0), iota((256, 256), 1)
    shift = (row < 128) & (((col < 128) & (row == col + 1)) | ((col >= 128) & (row + 129 == col)))
    edge = ((row >= 160) & (row < 192) & (col == 127)) | ((row >= 128) & (row < 160) & (col == 128))
    move[...] = jnp.where(shift | edge, 1.0, 0.0).astype(BF16)
    end = ((row % 128 == 127) & (col % 128 < 32)) | ((row % 128 == 0) & (col % 128 >= 32) & (col % 128 < 64))
    end = end & (row // 128 == col // 128)
    ends[...] = jnp.where(end, 1.0, 0.0).astype(BF16)
    end = (row % 128 == 127) & (row // 128 == col // 128)
    every[...] = jnp.where(end, 1.0, 0.0).astype(BF16)
    col = iota((128, 128), 1)
    to_first[...] = jnp.where(col == 0, 1.0, 0.0).astype(BF16)

    for copy in small:
        copy.wait()
    cn_in.start()

    columns = [jnp.zeros((TLAT, TLON), F32) for _ in range(FIELDS)]
    cell_row, cell_col = cells[...] >> 7, cells[...] & 127
    number = iota((128, 128), 0).astype(I16)
    for q in range(CHUNKS):
        in_row = number[:TLAT] == spread_row(cell_row[q : q + 1], I16, TLAT)
        in_col = one_hot(number == spread_row(cell_col[q : q + 1], I16, TLON))
        weighted = []
        for t in range(FIELDS):
            for part in parts_of(misfit[t, q : q + 1, :], 2):
                weighted.append(select(in_row, part.astype(F32), TLAT))
        placed = dot_nt(jnp.concatenate(weighted, axis=0), in_col)
        for t in range(FIELDS):
            base = 2 * t * TLAT
            columns[t] += placed[base : base + TLAT] + placed[base + TLAT : base + 2 * TLAT]
    for t in range(FIELDS):
        area[t, 8 : 8 + TLAT, :] = columns[t]

    ens_in.start()

    area[5, 8 : 8 + TLAT, :] = ce[0]
    area[6, 8 : 8 + TLAT, :] = cn[0, 8 : 8 + TLAT, :]
    first = jnp.zeros((TLAT, TLON), F32)
    final = jnp.zeros((TLAT, TLON), F32)
    for n in range(EXT):
        value = area[n, 8 : 8 + TLAT, :]
        here = (lane >= 4 * n) & (lane < 4 * n + 4)
        first = jnp.where(here, pltpu.roll(value, 4 * n, 1) if n else value, first)
        final = jnp.where(here, pltpu.roll(value, 4 * n + 4, 1), final)
    pack_w[...] = first
    pack_e[...] = final

    pl.semaphore_wait(barrier, len(peers))

    east = {"lon": shift_lon(1), "lat": lat}
    west = {"lon": shift_lon(-1), "lat": lat}
    north = {"lon": lon, "lat": shift_lat(1)}
    south = {"lon": lon, "lat": shift_lat(-1)}
    mid, low8, high8 = pl.ds(8, TLAT), pl.ds(0, 8), pl.ds(TLAT + 8, 8)
    edges = [
        remote(area.at[:, pl.ds(TLAT, 8), :], area.at[:, low8, :], north),
        remote(area.at[:, pl.ds(8, 8), :], area.at[:, high8, :], south),
        remote(pack_e, halo_w.at[mid, :], east),
        remote(pack_w, halo_e.at[mid, :], west),
        remote(pack_e.at[pl.ds(TLAT - 8, 8), :], halo_w.at[low8, :], {"lon": shift_lon(1), "lat": shift_lat(1)}),
        remote(pack_e.at[pl.ds(0, 8), :], halo_w.at[high8, :], {"lon": shift_lon(1), "lat": shift_lat(-1)}),
        remote(pack_w.at[pl.ds(TLAT - 8, 8), :], halo_e.at[low8, :], {"lon": shift_lon(-1), "lat": shift_lat(1)}),
        remote(pack_w.at[pl.ds(0, 8), :], halo_e.at[high8, :], {"lon": shift_lon(-1), "lat": shift_lat(-1)}),
    ]
    for copy in edges:
        copy.start()

    ce_in.wait()

    tip_columns = jnp.zeros((TLAT, TLON), F32)
    for k in range(0, LEV, KG):
        faces = [ce[k + i].astype(BF16) for i in range(KG)]
        pairs = [jnp.concatenate(faces[i : i + 2], axis=1) for i in range(0, KG, 2)]
        tips = dot_nn(jnp.concatenate(pairs, axis=0), every[...])
        for i in range(KG):
            tip = tips[i // 2 * TLAT : (i // 2 + 1) * TLAT, i % 2 * TLON : (i % 2 + 1) * TLON]
            tip_columns = jnp.where(lane == k + i, tip, tip_columns)
    cpack[...] = tip_columns
    cn_in.wait()
    cn_rows = cn.reshape(LEV * (TLAT + 8), TLON)
    last_row = cn_rows[pl.ds(TLAT + 7, LEV, stride=TLAT + 8), :] * jnp.where(lat < NLAT - 1, 1.0, 0.0)
    crow[...] = last_row
    cn_rows[pl.ds(TLAT + 7, LEV, stride=TLAT + 8), :] = last_row
    courants = [remote(crow, crhalo, north), remote(cpack, chalo, east)]
    for copy in courants:
        copy.start()

    total = jnp.zeros((128, 128), F32)
    slot1 = jnp.zeros((128, 128), F32)
    slot2 = jnp.zeros((128, 128), F32)
    before = jnp.where(iota((128, 128), 0) < iota((128, 128), 1), 1.0, 0.0).astype(BF16)
    ones = jnp.ones((128, 128), BF16)
    src, dst = psrc[...], pdst[...]
    s_lon, s_lat = src >> 8, (src >> 5) & 7
    s_x, s_y, s_z = (s_lon >> 1) & 3, (s_lat & 1) * 2 + (s_lon >> 3), s_lat >> 1
    s_slot = jnp.where((s_lon & 1) == 0, s_z * 16 + s_y * 4 + s_x, s_x * 16 + s_z * 4 + s_y)
    key1 = ((s_lon & 1) * 128 + ((src >> 3) & 3) * 32 + (dst & 31)).astype(F32)
    key2_high, key2_low = (s_slot * 8).astype(F32), (src & 7).astype(F32)
    tile = dst >> 5
    for q in range(CHUNKS):
        at = slice(q, q + 1)
        here = iota((128, 128), 0) == tile[at]
        mine = number == spread_row(tile[at], I16, 128)
        mark = one_hot(mine)
        count = dot_nn(mark, before) + total
        total += dot_nn(mark, ones)
        rank = jnp.sum(jnp.where(here, count, 0.0), axis=0, keepdims=True).astype(I32)
        at_low = one_hot(number == spread_row(rank, I16, 128))
        at_high = one_hot(number == spread_row(rank + 64, I16, 128))
        slot1 += dot_nt(select(mine, key1[at], 128), at_low)
        slot1 += dot_nt(select(mine, key2_high[at], 128), at_high)
        slot1 += dot_nt(select(mine, key2_low[at], 128), at_high)
        slot2 += dot_nt(select(mine, taper[at, :], 128), at_low)
    for d in range(NLON):
        slots1[d, 0] = slot1[d * 8 : d * 8 + 8]
        slots1[d, 1] = slot2[d * 8 : d * 8 + 8]

    routes = [
        remote(slots1.at[shift_lon(i)], route1.at[lon], {"lon": shift_lon(i), "lat": lat})
        for i in range(1, NLON)
    ]
    for copy in routes:
        copy.start()

    for copy in edges[:4]:
        copy.wait_recv()
    base = area[0, 8 : 8 + TLAT, :]
    shifted[0] = base
    shifted[1] = jnp.where(lane == 127, pltpu.roll(halo_e[8 : 8 + TLAT, :], 127, 1), pltpu.roll(base, 127, 1))
    shifted[2] = jnp.where(lane == 0, pltpu.roll(halo_w[8 : 8 + TLAT, :], 125, 1), pltpu.roll(base, 1, 1))
    shifted[3] = area[0, 9 : 9 + TLAT, :]
    shifted[4] = area[0, 7 : 7 + TLAT, :]

    for copy in courants:
        copy.wait_recv()
    cn_rows[pl.ds(7, LEV, stride=TLAT + 8), :] = crhalo[...] * jnp.where(lat > 0, 1.0, 0.0)
    field_rows = field.reshape(LEV * ROWS, TLON)

    def block(t, g, halo, kb, pack):
        base = g * KG + kb * LEVELS
        if t > 1:
            rows = []
            for i in range(LEVELS):
                mine = jnp.where(lane32 == kb * LEVELS + i, halo, 0.0).astype(BF16)
                rows.append(jnp.concatenate([field16[base + i], mine], axis=1))
            moved = dot_nn(jnp.concatenate(rows, axis=0), move[...])
        else:
            rows = [jnp.where(lane == base + i, halo, 0.0).astype(BF16) for i in range(LEVELS)]
            moved = dot_nn(jnp.concatenate(rows, axis=0), to_first[...])
        rounded = []
        for i in range(LEVELS):
            k = base + i
            kk = kern[k]
            if t == 1:
                faces = ce[k]
                pe = jnp.maximum(faces, 0.0)
                behind = jnp.where(lane == 0, moved[i * TLAT : (i + 1) * TLAT], pltpu.roll(faces, 1, 1))
                w = jnp.minimum(behind, 0.0)
                pn = jnp.maximum(cn[k, 8 : 8 + TLAT, :], 0.0)
                s = jnp.minimum(cn[k, 7 : 7 + TLAT, :], 0.0)
                c = (1.0 - pe) + w - pn + s
                ce[k] = pe
                cn[k, 8 : 8 + TLAT, :] = pn
                aw[k], asn[k], c0[k] = w, s, c
                new = kk * (
                    c * shifted[0] + pe * shifted[1] - w * shifted[2] + pn * shifted[3] - s * shifted[4]
                    + area[1, 8 : 8 + TLAT, :]
                )
            else:
                level_rows = slice(i * TLAT, (i + 1) * TLAT)
                new = (
                    c0[k] * field[k, 8 : 8 + TLAT, :]
                    + ce[k] * moved[level_rows, :TLON] - aw[k] * moved[level_rows, TLON:]
                    + cn[k, 8 : 8 + TLAT, :] * field[k, 9 : 9 + TLAT, :]
                    - asn[k] * field[k, 7 : 7 + TLAT, :] + kk * area[t, 8 : 8 + TLAT, :]
                )
            if t == 4:
                last[k] = new
                continue
            field[k, 8 : 8 + TLAT, :] = new
            new16 = new.astype(BF16)
            field16[k] = new16
            rounded.append(new16)
        if t == 4:
            return pack
        pairs = [jnp.concatenate(rounded[i : i + 2], axis=1) for i in range(0, LEVELS, 2)]
        tips = dot_nn(jnp.concatenate(pairs, axis=0), ends[...])
        for i in range(LEVELS):
            tip = tips[i // 2 * TLAT : (i // 2 + 1) * TLAT, i % 2 * TLON : (i % 2 + 1) * TLON]
            pack = jnp.where(lane32 == kb * LEVELS + i, tip, pack)
        return pack

    sent = {}
    outs = []

    def run_group(t, g):
        start = g * KG * ROWS
        halo = chalo[...]
        if t > 1:
            for copy in sent[t - 1, g]:
                copy.wait_recv()
            field_rows[pl.ds(start + 7, KG, stride=ROWS), :] = frhalo_s[t - 2, g]
            field_rows[pl.ds(start + 8 + TLAT, KG, stride=ROWS), :] = frhalo_n[t - 2, g]
            halo = jnp.where(lane < 32, fhalo_w[t - 2, g], fhalo_e[t - 2, g])
        pack = block(t, g, halo, 0, jnp.zeros((TLAT, TLON), F32))
        if t == 4:
            levels = pl.ds(g * KG, KG)
            outs.append(pltpu.make_async_copy(last.at[levels], out_hbm.at[levels], out_sem.at[g]))
            outs[-1].start()
            return
        fpack[t - 1, g] = pack
        frow_n[t - 1, g] = field_rows[pl.ds(start + 7 + TLAT, KG, stride=ROWS), :]
        frow_s[t - 1, g] = field_rows[pl.ds(start + 8, KG, stride=ROWS), :]
        sent[t, g] = [
            remote(frow_n.at[t - 1, g], frhalo_s.at[t - 1, g], north),
            remote(frow_s.at[t - 1, g], frhalo_n.at[t - 1, g], south),
            remote(fpack.at[t - 1, g], fhalo_w.at[t - 1, g], east),
            remote(fpack.at[t - 1, g], fhalo_e.at[t - 1, g], west),
        ]
        for copy in sent[t, g]:
            copy.start()

    run_group(1, 0)
    run_group(1, 1)
    route1[lon] = slots1[lon]
    for copy in routes:
        copy.wait_recv()
    for n in range(2):
        for a in range(NLAT):
            slots2[a, n] = jnp.concatenate([route1[d, n, a : a + 1, :] for d in range(NLON)], axis=0)
    routes2 = [
        remote(slots2.at[shift_lat(i)], route2.at[lat], {"lon": lon, "lat": shift_lat(i)})
        for i in range(1, NLAT)
    ]
    for copy in routes2:
        copy.start()
    route2[lat] = slots2[lat]

    for copy in edges[4:]:
        copy.wait_recv()

    wide_lane = iota((ROWS, TLON), 1)

    def widened(n):
        from_east = halo_e[...] if n == 0 else pltpu.roll(halo_e[...], 128 - 4 * n, 1)
        from_west = pltpu.roll(halo_w[...], 124 - 4 * n, 1)
        side = jnp.where(wide_lane < 64, from_east, from_west)
        return jnp.concatenate([area[n], side], axis=1)

    def up(v, axis):
        return pltpu.roll(v, v.shape[axis] - 1, axis)

    def down(v, axis):
        return pltpu.roll(v, 1, axis)

    forced = [widened(t) for t in range(FIELDS)]
    east0 = widened(5)
    global_row = lat * TLAT - 8 + iota((ROWS, 2 * TLON), 0)
    inside = (global_row >= 0) & (global_row < NLAT * TLAT - 1)
    north0 = jnp.where(inside, widened(6), 0.0)
    pe0, pn0 = jnp.maximum(east0, 0.0), jnp.maximum(north0, 0.0)
    aw0, as0 = -jnp.minimum(down(east0, 1), 0.0), -jnp.minimum(down(north0, 0), 0.0)
    c00 = 1.0 - pe0 - aw0 - pn0 - as0
    k0 = kern[0]
    level = k0 * forced[0]
    surface_wide = level
    for t in range(1, FIELDS):
        level = (
            c00 * level + pe0 * up(level, 1) + aw0 * down(level, 1)
            + pn0 * up(level, 0) + as0 * down(level, 0) + k0 * forced[t]
        )
        surface_wide = surface_wide + level
    surface = surface_wide[8 : 8 + TLAT, :TLON]
    prior[...] = surface

    ens_in.wait()
    rounded = surface.astype(BF16).astype(F32)

    @pl.loop(0, MEM)
    def _(m):
        product = ens[m].astype(F32) * rounded
        for r in range(4):
            at = pl.multiple_of((r * MEM + m) * 8, 8)
            partial[pl.ds(at, 8), :] = product[r * 16 : r * 16 + 8] + product[r * 16 + 8 : r * 16 + 16]

    row_sums = partial[pl.ds(0, 256, stride=8), :]
    for s in range(1, 8):
        row_sums += partial[pl.ds(s, 256, stride=8), :]
    in_block = jnp.where(iota((8, TLON), 0) == iota((8, TLON), 1) // BLK, 1.0, 0.0).astype(BF16)
    own[...] = sum(dot_nt(in_block, part) for part in parts_of(row_sums, 3))

    slot = jnp.where(core == 0, z * 16 + y * 4 + x, x * 16 + z * 4 + y)
    sibling = device(x, y, z, 1 - core)
    group = pl.ds(slot // 16 * 16, 16)
    plane = [
        remote(own, table.at[core, slot], plane_peer(i, j))
        for i in (2, 1, 3, 0) for j in (2, 1, 3, 0) if i or j
    ]
    for copy in plane:
        copy.start()
    table[core, slot] = own[...]
    shares, line = [], []

    def gather_line():
        for copy in plane:
            copy.wait_recv()
        line.extend(remote(table.at[core, group], table.at[core, group], line_peer(i)) for i in (2, 1, 3))
        shares.append(remote(table.at[core, group], table.at[core, group], sibling))
        for copy in line + shares:
            copy.start()

    def share_line():
        for n, i in enumerate((1, 3, 2)):
            line[(1, 2, 0)[n]].wait_recv()
            rows = pl.ds((slot // 16 + (4 - i)) % 4 * 16, 16)
            copy = remote(table.at[core, rows], table.at[core, rows], sibling)
            copy.start()
            shares.append(copy)

    run_group(1, 2)

    run_group(2, 0)
    run_group(2, 1)
    run_group(2, 2)

    for copy in routes2:
        copy.wait_recv()
    half = iota((16, 128), 1) < 64
    for a in range(4):
        one, two = route2[a, 0], route2[a + 4, 0]
        at = slice(a * 16, a * 16 + 16)
        keys[0, at] = jnp.where(half, one, pltpu.roll(two, 64, 1))
        keys[1, at] = jnp.where(half, pltpu.roll(one, 64, 1), two)
        keys[2, at] = jnp.where(half, route2[a, 1], pltpu.roll(route2[a + 4, 1], 64, 1))
    weights[...] = jnp.zeros_like(weights)

    def add_weights(i, carry):
        at = pl.ds(pl.multiple_of(i * 8, 8), 8)
        key1, key2, weight = keys[0, at, :].astype(I32), keys[1, at, :].astype(I32), keys[2, at, :]
        number = iota((128, 128), 0).astype(I16)
        lhs, rhs = [], []
        for u in range(8):
            one = slice(u, u + 1)
            match = [number == spread_row(key1[one] - r, I16, 128) for r in (0, 128)]
            lhs.append(jnp.concatenate([select(m, weight[one], 128) for m in match], axis=0))
            match = [number == spread_row(key2[one] - r, I16, 128) for r in (0, 128, 256, 384)]
            rhs.append(jnp.concatenate([one_hot(m) for m in match], axis=0))
        weights[...] += dot_nt(jnp.concatenate(lhs, axis=1), jnp.concatenate(rhs, axis=1))
        return carry

    lax.fori_loop(0, 4, add_weights, 0)
    gather_line()

    run_group(3, 0)
    run_group(3, 1)
    run_group(3, 2)

    lax.fori_loop(4, 8, add_weights, 0)
    w_parts = parts_of(weights[...], 2)
    weights16[0] = w_parts[0]
    weights16[1] = w_parts[1]

    run_group(4, 0)
    share_line()
    run_group(4, 1)
    run_group(4, 2)

    combined4 = jnp.zeros((128, 256), F32)
    for half in (core, 1 - core):
        if half is not core:
            for copy in shares:
                copy.wait_recv()
        for q in range(2):
            t_high, t_low = parts_of(table[half, q * 32 : q * 32 + 32].reshape(256, 256), 2)
            w_rows = pl.ds(pl.multiple_of(half * 128, 128), 128)
            w_high, w_low = (weights16[n, w_rows, q * 256 : q * 256 + 256] for n in range(2))
            combined4 += dot_nn(w_high, t_high) + dot_nn(w_high, t_low) + dot_nn(w_low, t_high)
    combined = combined4[:32, :64]
    for r in range(1, 4):
        combined += combined4[r * 32 : (r + 1) * 32, r * 64 : (r + 1) * 64]
    for r in range(4):
        ycol[r] = dot_tn(combined[r * 8 : r * 8 + 8].astype(BF16), in_block)

    def add_member(m, acc):
        rows = [jnp.broadcast_to(ycol[r, pl.ds(m, 1), :], (BLK, TLON)) for r in range(4)]
        return acc + ens[m].astype(F32) * jnp.concatenate(rows, axis=0)

    prior[...] = lax.fori_loop(0, MEM, add_member, var_ref[...] * prior[...], unroll=8)
    outs.append(pltpu.make_async_copy(prior, prior_hbm, out_sem.at[GROUPS]))
    outs[-1].start()

    for copy in outs:
        copy.wait()
    flights = edges + courants + routes + routes2 + plane + line + shares
    flights += [copy for group in sent.values() for copy in group]
    for copy in flights:
        copy.wait_send()


def hand_over(field, prior, field_out, prior_out, field_held, prior_held, in_sem, out_sem):
    steps = LEV // PIECES
    parts = [(prior, prior_held, prior_out)]
    for n in range(PIECES):
        levels = pl.ds(n * steps, steps)
        parts.append((field.at[levels], field_held.at[levels], field_out.at[levels]))
    loads = [
        pltpu.make_async_copy(src, held, in_sem.at[n]) for n, (src, held, _) in enumerate(parts)
    ]
    stores = [
        pltpu.make_async_copy(held, dst, out_sem.at[n]) for n, (_, held, dst) in enumerate(parts)
    ]
    for load in loads:
        load.start()
    for load, store in zip(loads, stores):
        load.wait()
        store.start()
    for store in stores:
        store.wait()


def per_device(ce, cn, cells, misfit, kern, ens, psrc, pdst, taper, var):
    hbm = pl.BlockSpec(memory_space=pl.ANY)
    tile = (TLAT, TLON)
    field, prior = pl.pallas_call(
        kernel,
        out_shape=(
            jax.ShapeDtypeStruct((LEV,) + tile, F32),
            jax.ShapeDtypeStruct(tile, F32),
        ),
        in_specs=[hbm] * 10,
        out_specs=(hbm, hbm),
        scratch_shapes=[
            pltpu.VMEM((8, 128), I32),
            pltpu.VMEM((FIELDS, 8, 128), F32),
            pltpu.SMEM((LEV,), F32),
            pltpu.VMEM((8, 128), I32),
            pltpu.VMEM((8, 128), I32),
            pltpu.VMEM((8, 128), F32),
            pltpu.VMEM(tile, F32),
            pltpu.VMEM((LEV,) + tile, F32),
            pltpu.VMEM((LEV, TLAT + 8, TLON), F32),
            pltpu.VMEM((LEV,) + tile, F32),
            pltpu.VMEM((LEV,) + tile, F32),
            pltpu.VMEM((LEV,) + tile, F32),
            pltpu.VMEM((LEV, ROWS, TLON), F32),
            pltpu.VMEM((LEV,) + tile, BF16),
            pltpu.VMEM((LEV,) + tile, F32),
            pltpu.VMEM((MEM,) + tile, BF16),
            pltpu.VMEM((EXT, ROWS, TLON), F32),
            pltpu.VMEM((ROWS, TLON), F32),
            pltpu.VMEM((ROWS, TLON), F32),
            pltpu.VMEM(tile, F32),
            pltpu.VMEM(tile, F32),
            pltpu.VMEM(tile, F32),
            pltpu.VMEM(tile, F32),
            pltpu.VMEM((LEV, TLON), F32),
            pltpu.VMEM((LEV, TLON), F32),
            pltpu.VMEM((5,) + tile, F32),
        ]
        + [pltpu.VMEM((ROUNDS, GROUPS) + tile, F32) for _ in range(3)]
        + [pltpu.VMEM((256, 256), BF16) for _ in range(3)]
        + [pltpu.VMEM((128, 128), BF16)]
        + [pltpu.VMEM((ROUNDS, GROUPS, KG, TLON), F32) for _ in range(4)]
        + [
            pltpu.VMEM((NLON, 2, 8, 128), F32),
            pltpu.VMEM((NLON, 2, 8, 128), F32),
            pltpu.VMEM((NLAT, 2, 16, 128), F32),
            pltpu.VMEM((NLAT, 2, 16, 128), F32),
            pltpu.VMEM((3, 64, 128), F32),
            pltpu.VMEM((256, 512), F32),
            pltpu.VMEM((2, 256, 512), BF16),
            pltpu.VMEM((256 * 8, TLON), F32),
            pltpu.VMEM((8, 256), F32),
            pltpu.VMEM((2, 64, 8, 256), F32),
            pltpu.VMEM((4, MEM, TLON), F32),
            pltpu.VMEM(tile, F32),
            pltpu.SemaphoreType.DMA((12,)),
            pltpu.SemaphoreType.DMA((GROUPS + 1,)),
            pltpu.SemaphoreType.DMA((COPIES,)),
            pltpu.SemaphoreType.DMA((COPIES,)),
        ],
        compiler_params=pltpu.CompilerParams(
            collective_id=0, has_side_effects=True, vmem_limit_bytes=60 * 1024 * 1024
        ),
    )(
        ce, cn, cells.reshape(8, 128), misfit.reshape(FIELDS, 8, 128), kern, ens,
        psrc.reshape(8, 128), pdst.reshape(8, 128), taper.reshape(8, 128), var,
    )
    return pl.pallas_call(
        hand_over,
        out_shape=(
            jax.ShapeDtypeStruct((LEV,) + tile, F32),
            jax.ShapeDtypeStruct(tile, F32),
        ),
        in_specs=[hbm] * 2,
        out_specs=(hbm, hbm),
        scratch_shapes=[
            pltpu.VMEM((LEV,) + tile, F32),
            pltpu.VMEM(tile, F32),
            pltpu.SemaphoreType.DMA((PIECES + 1,)),
            pltpu.SemaphoreType.DMA((PIECES + 1,)),
        ],
        compiler_params=pltpu.CompilerParams(vmem_limit_bytes=60 * 1024 * 1024),
    )(field, prior)


def solution(mesh):
    in_specs = (
        P(None, "lat", "lon"),
        P(None, "lat", "lon"),
        P("lat", "lon", None),
        P(None, "lat", "lon", None),
        P(),
        P(None, "lat", "lon"),
        P(("lon", "lat")),
        P(("lon", "lat")),
        P(("lon", "lat")),
        P("lat", "lon"),
    )
    out_specs = (P(None, "lat", "lon"), P("lat", "lon"))
    return jax.shard_map(
        per_device, mesh=mesh, in_specs=in_specs, out_specs=out_specs, check_vma=False
    )
```

```python
import jax
import jax.numpy as jnp
from jax import lax
from jax.experimental import pallas as pl
from jax.experimental.pallas import tpu as pltpu
from jax.sharding import PartitionSpec as P

MESH = pl.DeviceIdType.MESH
F32, BF16, I32, I16 = jnp.float32, jnp.bfloat16, jnp.int32, jnp.int16

TLAT, TLON, LEV, BLK, MEM = 64, 128, 72, 16, 64
NLON, NLAT = 16, 8
FIELDS = 5
EXT = 7
ROWS = TLAT + 16
GROUPS = 3
PIECES = 8
KG = LEV // GROUPS
LEVELS = KG
ROUNDS = 3
CHUNKS = 8
COPIES = 8 + 2 + 4 * ROUNDS * GROUPS + 15 + 7 + 15 + 1 + 3 + 3


def iota(shape, dim):
    return lax.broadcasted_iota(I32, shape, dim)


def dot_nt(a, b):
    return lax.dot_general(a, b, (((1,), (1,)), ((), ())), preferred_element_type=F32)


def dot_tn(a, b):
    return lax.dot_general(a, b, (((0,), (0,)), ((), ())), preferred_element_type=F32)


def dot_nn(a, b):
    return lax.dot_general(a, b, (((1,), (0,)), ((), ())), preferred_element_type=F32)


def spread_row(row, dtype, rows):
    few = jnp.broadcast_to(row, (16, 128)).astype(dtype)
    return jnp.concatenate([few] * (rows // 16), axis=0)


def select(mask, row, rows):
    return jnp.where(mask, spread_row(row, BF16, rows), jnp.zeros((), BF16))


def one_hot(mask):
    return jnp.where(mask, jnp.ones((), BF16), jnp.zeros((), BF16))


def parts_of(x, count):
    parts = []
    for _ in range(count):
        part = x.astype(BF16)
        parts.append(part)
        x = x - part.astype(F32)
    return parts


def kernel(
    ce_hbm, cn_hbm, cells_hbm, misfit_hbm, kern_hbm, ens_hbm, psrc_hbm, pdst_hbm, taper_hbm, var_hbm,
    out_hbm, prior_hbm,
    cells, misfit, kern, psrc, pdst, taper, var_ref,
    ce, cn, aw, asn, c0, field, field16, last, ens, area, halo_e, halo_w, pack_e, pack_w,
    cpack, chalo, crow, crhalo, shifted,
    fpack, fhalo_e, fhalo_w, move, ends, every, to_first, frow_n, frow_s, frhalo_n, frhalo_s,
    slots1, route1, slots2, route2, keys, weights, weights16,
    partial, own, table, ycol, prior,
    local_sem, out_sem, send_sem, recv_sem,
):
    lon, lat = lax.axis_index("lon"), lax.axis_index("lat")
    core, x, y_lo = lon % 2, (lon // 2) % 4, lon // 8
    z, y_hi = lat // 2, lat % 2
    y = y_hi * 2 + y_lo

    def shift_lon(s):
        return (lon + s + NLON) % NLON

    def shift_lat(s):
        return (lat + s + NLAT) % NLAT

    def device(xx, yy, zz, cc):
        return {"lon": (yy % 2) * 8 + xx * 2 + cc, "lat": zz * 2 + yy // 2}

    rest = pl.ds(1, LEV - 1)
    first_axis, second_axis, third_axis = (1 - core, core, 0), (0, 1 - core, core), (core, 0, 1 - core)

    def plane_peer(i, j):
        place = [(v + i * a + j * b) % 4 for v, a, b in zip((x, y, z), first_axis, second_axis)]
        return device(*place, core)

    def line_peer(i):
        return device(*[(v + i * a) % 4 for v, a in zip((x, y, z), third_axis)], core)

    ce_in = pltpu.make_async_copy(ce_hbm.at[rest], ce.at[rest], local_sem.at[0])
    cn_in = pltpu.make_async_copy(cn_hbm.at[rest], cn.at[rest, pl.ds(8, TLAT), :], local_sem.at[1])
    ens_in = pltpu.make_async_copy(ens_hbm, ens, local_sem.at[2])
    small = [
        pltpu.make_async_copy(src, dst, local_sem.at[3 + n])
        for n, (src, dst) in enumerate((
            (cells_hbm, cells), (misfit_hbm, misfit), (kern_hbm, kern), (psrc_hbm, psrc),
            (pdst_hbm, pdst), (taper_hbm, taper), (var_hbm, var_ref),
            (ce_hbm.at[0], ce.at[0]), (cn_hbm.at[0], cn.at[0, pl.ds(8, TLAT), :]),
        ))
    ]
    for copy in small + [ce_in]:
        copy.start()

    barrier = pltpu.get_barrier_semaphore()
    peers = [{"lon": shift_lon(i), "lat": lat} for i in range(1, NLON)]
    peers += [{"lon": lon, "lat": shift_lat(i)} for i in range(1, NLAT)]
    peers += [plane_peer(i, j) for i in range(4) for j in range(4) if i or j]
    peers += [{"lon": shift_lon(i), "lat": shift_lat(j)} for i in (-1, 1) for j in (-1, 1)]
    for peer in peers:
        pl.semaphore_signal(barrier, inc=1, device_id=peer, device_id_type=MESH)

    used = [0]

    def remote(src, dst, peer):
        n = used[0]
        used[0] += 1
        return pltpu.make_async_remote_copy(
            src_ref=src, dst_ref=dst, send_sem=send_sem.at[n], recv_sem=recv_sem.at[n],
            device_id=peer, device_id_type=MESH,
        )

    lane = iota((TLAT, TLON), 1)
    lane32 = lane % 32

    for copy in small:
        copy.wait()
    cn_in.start()

    columns = [jnp.zeros((TLAT, TLON), F32) for _ in range(FIELDS)]
    cell_row, cell_col = cells[...] >> 7, cells[...] & 127
    number = iota((128, 128), 0).astype(I16)
    for q in range(CHUNKS):
        in_row = number[:TLAT] == spread_row(cell_row[q : q + 1], I16, TLAT)
        in_col = one_hot(number == spread_row(cell_col[q : q + 1], I16, TLON))
        weighted = []
        for t in range(FIELDS):
            for part in parts_of(misfit[t, q : q + 1, :], 2):
                weighted.append(select(in_row, part.astype(F32), TLAT))
        placed = dot_nt(jnp.concatenate(weighted, axis=0), in_col)
        for t in range(FIELDS):
            base = 2 * t * TLAT
            columns[t] += placed[base : base + TLAT] + placed[base + TLAT : base + 2 * TLAT]
    for t in range(FIELDS):
        area[t, 8 : 8 + TLAT, :] = columns[t]

    ens_in.start()

    area[5, 8 : 8 + TLAT, :] = ce[0]
    area[6, 8 : 8 + TLAT, :] = cn[0, 8 : 8 + TLAT, :]
    first = jnp.zeros((TLAT, TLON), F32)
    final = jnp.zeros((TLAT, TLON), F32)
    for n in range(EXT):
        value = area[n, 8 : 8 + TLAT, :]
        here = (lane >= 4 * n) & (lane < 4 * n + 4)
        first = jnp.where(here, pltpu.roll(value, 4 * n, 1) if n else value, first)
        final = jnp.where(here, pltpu.roll(value, 4 * n + 4, 1), final)
    pack_w[...] = first
    pack_e[...] = final

    pl.semaphore_wait(barrier, len(peers))

    east = {"lon": shift_lon(1), "lat": lat}
    west = {"lon": shift_lon(-1), "lat": lat}
    north = {"lon": lon, "lat": shift_lat(1)}
    south = {"lon": lon, "lat": shift_lat(-1)}
    mid, low8, high8 = pl.ds(8, TLAT), pl.ds(0, 8), pl.ds(TLAT + 8, 8)
    edges = [
        remote(area.at[:, pl.ds(TLAT, 8), :], area.at[:, low8, :], north),
        remote(area.at[:, pl.ds(8, 8), :], area.at[:, high8, :], south),
        remote(pack_e, halo_w.at[mid, :], east),
        remote(pack_w, halo_e.at[mid, :], west),
        remote(pack_e.at[pl.ds(TLAT - 8, 8), :], halo_w.at[low8, :], {"lon": shift_lon(1), "lat": shift_lat(1)}),
        remote(pack_e.at[pl.ds(0, 8), :], halo_w.at[high8, :], {"lon": shift_lon(1), "lat": shift_lat(-1)}),
        remote(pack_w.at[pl.ds(TLAT - 8, 8), :], halo_e.at[low8, :], {"lon": shift_lon(-1), "lat": shift_lat(1)}),
        remote(pack_w.at[pl.ds(0, 8), :], halo_e.at[high8, :], {"lon": shift_lon(-1), "lat": shift_lat(-1)}),
    ]
    for copy in edges:
        copy.start()

    row, col = iota((256, 256), 0), iota((256, 256), 1)
    end = (row % 128 == 127) & (row // 128 == col // 128)
    every[...] = jnp.where(end, 1.0, 0.0).astype(BF16)
    ce_in.wait()

    tip_columns = jnp.zeros((TLAT, TLON), F32)
    for k in range(0, LEV, KG):
        faces = [ce[k + i].astype(BF16) for i in range(KG)]
        pairs = [jnp.concatenate(faces[i : i + 2], axis=1) for i in range(0, KG, 2)]
        tips = dot_nn(jnp.concatenate(pairs, axis=0), every[...])
        for i in range(KG):
            tip = tips[i // 2 * TLAT : (i // 2 + 1) * TLAT, i % 2 * TLON : (i % 2 + 1) * TLON]
            tip_columns = jnp.where(lane == k + i, tip, tip_columns)
    cpack[...] = tip_columns
    cn_in.wait()
    cn_rows = cn.reshape(LEV * (TLAT + 8), TLON)
    last_row = cn_rows[pl.ds(TLAT + 7, LEV, stride=TLAT + 8), :] * jnp.where(lat < NLAT - 1, 1.0, 0.0)
    crow[...] = last_row
    cn_rows[pl.ds(TLAT + 7, LEV, stride=TLAT + 8), :] = last_row
    courants = [remote(crow, crhalo, north), remote(cpack, chalo, east)]
    for copy in courants:
        copy.start()

    total = jnp.zeros((128, 128), F32)
    slot1 = jnp.zeros((128, 128), F32)
    slot2 = jnp.zeros((128, 128), F32)
    before = jnp.where(iota((128, 128), 0) < iota((128, 128), 1), 1.0, 0.0).astype(BF16)
    ones = jnp.ones((128, 128), BF16)
    src, dst = psrc[...], pdst[...]
    s_lon, s_lat = src >> 8, (src >> 5) & 7
    s_x, s_y, s_z = (s_lon >> 1) & 3, (s_lat & 1) * 2 + (s_lon >> 3), s_lat >> 1
    s_slot = jnp.where((s_lon & 1) == 0, s_z * 16 + s_y * 4 + s_x, s_x * 16 + s_z * 4 + s_y)
    key1 = ((s_lon & 1) * 128 + ((src >> 3) & 3) * 32 + (dst & 31)).astype(F32)
    key2_high, key2_low = (s_slot * 8).astype(F32), (src & 7).astype(F32)
    tile = dst >> 5
    for q in range(CHUNKS):
        at = slice(q, q + 1)
        here = iota((128, 128), 0) == tile[at]
        mine = number == spread_row(tile[at], I16, 128)
        mark = one_hot(mine)
        count = dot_nn(mark, before) + total
        total += dot_nn(mark, ones)
        rank = jnp.sum(jnp.where(here, count, 0.0), axis=0, keepdims=True).astype(I32)
        at_low = one_hot(number == spread_row(rank, I16, 128))
        at_high = one_hot(number == spread_row(rank + 64, I16, 128))
        slot1 += dot_nt(select(mine, key1[at], 128), at_low)
        slot1 += dot_nt(select(mine, key2_high[at], 128), at_high)
        slot1 += dot_nt(select(mine, key2_low[at], 128), at_high)
        slot2 += dot_nt(select(mine, taper[at, :], 128), at_low)
    for d in range(NLON):
        slots1[d, 0] = slot1[d * 8 : d * 8 + 8]
        slots1[d, 1] = slot2[d * 8 : d * 8 + 8]

    routes = [
        remote(slots1.at[shift_lon(i)], route1.at[lon], {"lon": shift_lon(i), "lat": lat})
        for i in range(1, NLON)
    ]
    for copy in routes:
        copy.start()

    row, col = iota((256, 256), 0), iota((256, 256), 1)
    shift = (row < 128) & (((col < 128) & (row == col + 1)) | ((col >= 128) & (row + 129 == col)))
    edge = ((row >= 160) & (row < 192) & (col == 127)) | ((row >= 128) & (row < 160) & (col == 128))
    move[...] = jnp.where(shift | edge, 1.0, 0.0).astype(BF16)
    end = ((row % 128 == 127) & (col % 128 < 32)) | ((row % 128 == 0) & (col % 128 >= 32) & (col % 128 < 64))
    end = end & (row // 128 == col // 128)
    ends[...] = jnp.where(end, 1.0, 0.0).astype(BF16)
    col = iota((128, 128), 1)
    to_first[...] = jnp.where(col == 0, 1.0, 0.0).astype(BF16)

    for copy in edges[:4]:
        copy.wait_recv()
    base = area[0, 8 : 8 + TLAT, :]
    shifted[0] = base
    shifted[1] = jnp.where(lane == 127, pltpu.roll(halo_e[8 : 8 + TLAT, :], 127, 1), pltpu.roll(base, 127, 1))
    shifted[2] = jnp.where(lane == 0, pltpu.roll(halo_w[8 : 8 + TLAT, :], 125, 1), pltpu.roll(base, 1, 1))
    shifted[3] = area[0, 9 : 9 + TLAT, :]
    shifted[4] = area[0, 7 : 7 + TLAT, :]

    for copy in courants:
        copy.wait_recv()
    cn_rows[pl.ds(7, LEV, stride=TLAT + 8), :] = crhalo[...] * jnp.where(lat > 0, 1.0, 0.0)
    field_rows = field.reshape(LEV * ROWS, TLON)

    def block(t, g, halo, kb, pack):
        base = g * KG + kb * LEVELS
        if t > 1:
            rows = []
            for i in range(LEVELS):
                mine = jnp.where(lane32 == kb * LEVELS + i, halo, 0.0).astype(BF16)
                rows.append(jnp.concatenate([field16[base + i], mine], axis=1))
            moved = dot_nn(jnp.concatenate(rows, axis=0), move[...])
        else:
            rows = [jnp.where(lane == base + i, halo, 0.0).astype(BF16) for i in range(LEVELS)]
            moved = dot_nn(jnp.concatenate(rows, axis=0), to_first[...])
        rounded = []
        for i in range(LEVELS):
            k = base + i
            kk = kern[k]
            if t == 1:
                faces = ce[k]
                pe = jnp.maximum(faces, 0.0)
                behind = jnp.where(lane == 0, moved[i * TLAT : (i + 1) * TLAT], pltpu.roll(faces, 1, 1))
                w = jnp.minimum(behind, 0.0)
                pn = jnp.maximum(cn[k, 8 : 8 + TLAT, :], 0.0)
                s = jnp.minimum(cn[k, 7 : 7 + TLAT, :], 0.0)
                c = (1.0 - pe) + w - pn + s
                ce[k] = pe
                cn[k, 8 : 8 + TLAT, :] = pn
                aw[k], asn[k], c0[k] = w, s, c
                new = kk * (
                    c * shifted[0] + pe * shifted[1] - w * shifted[2] + pn * shifted[3] - s * shifted[4]
                    + area[1, 8 : 8 + TLAT, :]
                )
            else:
                level_rows = slice(i * TLAT, (i + 1) * TLAT)
                new = (
                    c0[k] * field[k, 8 : 8 + TLAT, :]
                    + ce[k] * moved[level_rows, :TLON] - aw[k] * moved[level_rows, TLON:]
                    + cn[k, 8 : 8 + TLAT, :] * field[k, 9 : 9 + TLAT, :]
                    - asn[k] * field[k, 7 : 7 + TLAT, :] + kk * area[t, 8 : 8 + TLAT, :]
                )
            if t == 4:
                last[k] = new
                continue
            field[k, 8 : 8 + TLAT, :] = new
            new16 = new.astype(BF16)
            field16[k] = new16
            rounded.append(new16)
        if t == 4:
            return pack
        pairs = [jnp.concatenate(rounded[i : i + 2], axis=1) for i in range(0, LEVELS, 2)]
        tips = dot_nn(jnp.concatenate(pairs, axis=0), ends[...])
        for i in range(LEVELS):
            tip = tips[i // 2 * TLAT : (i // 2 + 1) * TLAT, i % 2 * TLON : (i % 2 + 1) * TLON]
            pack = jnp.where(lane32 == kb * LEVELS + i, tip, pack)
        return pack

    sent = {}
    outs = []

    def run_group(t, g):
        start = g * KG * ROWS
        halo = chalo[...]
        if t > 1:
            for copy in sent[t - 1, g]:
                copy.wait_recv()
            field_rows[pl.ds(start + 7, KG, stride=ROWS), :] = frhalo_s[t - 2, g]
            field_rows[pl.ds(start + 8 + TLAT, KG, stride=ROWS), :] = frhalo_n[t - 2, g]
            halo = jnp.where(lane < 32, fhalo_w[t - 2, g], fhalo_e[t - 2, g])
        pack = block(t, g, halo, 0, jnp.zeros((TLAT, TLON), F32))
        if t == 4:
            levels = pl.ds(g * KG, KG)
            outs.append(pltpu.make_async_copy(last.at[levels], out_hbm.at[levels], out_sem.at[g]))
            outs[-1].start()
            return
        fpack[t - 1, g] = pack
        frow_n[t - 1, g] = field_rows[pl.ds(start + 7 + TLAT, KG, stride=ROWS), :]
        frow_s[t - 1, g] = field_rows[pl.ds(start + 8, KG, stride=ROWS), :]
        sent[t, g] = [
            remote(frow_n.at[t - 1, g], frhalo_s.at[t - 1, g], north),
            remote(frow_s.at[t - 1, g], frhalo_n.at[t - 1, g], south),
            remote(fpack.at[t - 1, g], fhalo_w.at[t - 1, g], east),
            remote(fpack.at[t - 1, g], fhalo_e.at[t - 1, g], west),
        ]
        for copy in sent[t, g]:
            copy.start()

    run_group(1, 0)
    run_group(1, 1)
    run_group(1, 2)

    route1[lon] = slots1[lon]
    for copy in routes:
        copy.wait_recv()
    for n in range(2):
        for a in range(NLAT):
            slots2[a, n] = jnp.concatenate([route1[d, n, a : a + 1, :] for d in range(NLON)], axis=0)
    routes2 = [
        remote(slots2.at[shift_lat(i)], route2.at[lat], {"lon": lon, "lat": shift_lat(i)})
        for i in range(1, NLAT)
    ]
    for copy in routes2:
        copy.start()
    route2[lat] = slots2[lat]

    for copy in edges[4:]:
        copy.wait_recv()

    wide_lane = iota((ROWS, TLON), 1)

    def widened(n):
        from_east = halo_e[...] if n == 0 else pltpu.roll(halo_e[...], 128 - 4 * n, 1)
        from_west = pltpu.roll(halo_w[...], 124 - 4 * n, 1)
        side = jnp.where(wide_lane < 64, from_east, from_west)
        return jnp.concatenate([area[n], side], axis=1)

    def up(v, axis):
        return pltpu.roll(v, v.shape[axis] - 1, axis)

    def down(v, axis):
        return pltpu.roll(v, 1, axis)

    forced = [widened(t) for t in range(FIELDS)]
    east0 = widened(5)
    global_row = lat * TLAT - 8 + iota((ROWS, 2 * TLON), 0)
    inside = (global_row >= 0) & (global_row < NLAT * TLAT - 1)
    north0 = jnp.where(inside, widened(6), 0.0)
    pe0, pn0 = jnp.maximum(east0, 0.0), jnp.maximum(north0, 0.0)
    aw0, as0 = -jnp.minimum(down(east0, 1), 0.0), -jnp.minimum(down(north0, 0), 0.0)
    c00 = 1.0 - pe0 - aw0 - pn0 - as0
    k0 = kern[0]
    level = k0 * forced[0]
    surface_wide = level
    for t in range(1, FIELDS):
        level = (
            c00 * level + pe0 * up(level, 1) + aw0 * down(level, 1)
            + pn0 * up(level, 0) + as0 * down(level, 0) + k0 * forced[t]
        )
        surface_wide = surface_wide + level
    surface = surface_wide[8 : 8 + TLAT, :TLON]
    prior[...] = surface

    ens_in.wait()
    rounded = surface.astype(BF16).astype(F32)

    @pl.loop(0, MEM)
    def _(m):
        product = ens[m].astype(F32) * rounded
        for r in range(4):
            at = pl.multiple_of((r * MEM + m) * 8, 8)
            partial[pl.ds(at, 8), :] = product[r * 16 : r * 16 + 8] + product[r * 16 + 8 : r * 16 + 16]

    row_sums = partial[pl.ds(0, 256, stride=8), :]
    for s in range(1, 8):
        row_sums += partial[pl.ds(s, 256, stride=8), :]
    in_block = jnp.where(iota((8, TLON), 0) == iota((8, TLON), 1) // BLK, 1.0, 0.0).astype(BF16)
    own[...] = sum(dot_nt(in_block, part) for part in parts_of(row_sums, 3))

    slot = jnp.where(core == 0, z * 16 + y * 4 + x, x * 16 + z * 4 + y)
    sibling = device(x, y, z, 1 - core)
    group = pl.ds(slot // 16 * 16, 16)
    plane = [
        remote(own, table.at[core, slot], plane_peer(i, j))
        for i in (2, 1, 3, 0) for j in (2, 1, 3, 0) if i or j
    ]
    for copy in plane:
        copy.start()
    table[core, slot] = own[...]
    shares, line = [], []

    def gather_line():
        for copy in plane:
            copy.wait_recv()
        line.extend(remote(table.at[core, group], table.at[core, group], line_peer(i)) for i in (2, 1, 3))
        shares.append(remote(table.at[core, group], table.at[core, group], sibling))
        for copy in line + shares:
            copy.start()

    def share_line():
        for n, i in enumerate((1, 3, 2)):
            line[(1, 2, 0)[n]].wait_recv()
            rows = pl.ds((slot // 16 + (4 - i)) % 4 * 16, 16)
            copy = remote(table.at[core, rows], table.at[core, rows], sibling)
            copy.start()
            shares.append(copy)

    run_group(2, 0)
    run_group(2, 1)
    run_group(2, 2)

    for copy in routes2:
        copy.wait_recv()
    half = iota((16, 128), 1) < 64
    for a in range(4):
        one, two = route2[a, 0], route2[a + 4, 0]
        at = slice(a * 16, a * 16 + 16)
        keys[0, at] = jnp.where(half, one, pltpu.roll(two, 64, 1))
        keys[1, at] = jnp.where(half, pltpu.roll(one, 64, 1), two)
        keys[2, at] = jnp.where(half, route2[a, 1], pltpu.roll(route2[a + 4, 1], 64, 1))
    weights[...] = jnp.zeros_like(weights)

    def add_weights(i, carry):
        at = pl.ds(pl.multiple_of(i * 8, 8), 8)
        key1, key2, weight = keys[0, at, :].astype(I32), keys[1, at, :].astype(I32), keys[2, at, :]
        number = iota((128, 128), 0).astype(I16)
        lhs, rhs = [], []
        for u in range(8):
            one = slice(u, u + 1)
            match = [number == spread_row(key1[one] - r, I16, 128) for r in (0, 128)]
            lhs.append(jnp.concatenate([select(m, weight[one], 128) for m in match], axis=0))
            match = [number == spread_row(key2[one] - r, I16, 128) for r in (0, 128, 256, 384)]
            rhs.append(jnp.concatenate([one_hot(m) for m in match], axis=0))
        weights[...] += dot_nt(jnp.concatenate(lhs, axis=1), jnp.concatenate(rhs, axis=1))
        return carry

    lax.fori_loop(0, 4, add_weights, 0)
    gather_line()

    run_group(3, 0)
    run_group(3, 1)
    run_group(3, 2)

    lax.fori_loop(4, 8, add_weights, 0)
    w_parts = parts_of(weights[...], 2)
    weights16[0] = w_parts[0]
    weights16[1] = w_parts[1]

    run_group(4, 0)
    share_line()
    run_group(4, 1)
    run_group(4, 2)

    combined4 = jnp.zeros((128, 256), F32)
    for half in (core, 1 - core):
        if half is not core:
            for copy in shares:
                copy.wait_recv()
        for q in range(2):
            t_high, t_low = parts_of(table[half, q * 32 : q * 32 + 32].reshape(256, 256), 2)
            w_rows = pl.ds(pl.multiple_of(half * 128, 128), 128)
            w_high, w_low = (weights16[n, w_rows, q * 256 : q * 256 + 256] for n in range(2))
            combined4 += dot_nn(w_high, t_high) + dot_nn(w_high, t_low) + dot_nn(w_low, t_high)
    combined = combined4[:32, :64]
    for r in range(1, 4):
        combined += combined4[r * 32 : (r + 1) * 32, r * 64 : (r + 1) * 64]
    for r in range(4):
        ycol[r] = dot_tn(combined[r * 8 : r * 8 + 8].astype(BF16), in_block)

    def add_member(m, acc):
        rows = [jnp.broadcast_to(ycol[r, pl.ds(m, 1), :], (BLK, TLON)) for r in range(4)]
        return acc + ens[m].astype(F32) * jnp.concatenate(rows, axis=0)

    prior[...] = lax.fori_loop(0, MEM, add_member, var_ref[...] * prior[...], unroll=8)
    outs.append(pltpu.make_async_copy(prior, prior_hbm, out_sem.at[GROUPS]))
    outs[-1].start()

    for copy in outs:
        copy.wait()
    flights = edges + courants + routes + routes2 + plane + line + shares
    flights += [copy for group in sent.values() for copy in group]
    for copy in flights:
        copy.wait_send()


def hand_over(field, prior, field_out, prior_out, field_held, prior_held, in_sem, out_sem):
    steps = LEV // PIECES
    parts = [(prior, prior_held, prior_out)]
    for n in range(PIECES):
        levels = pl.ds(n * steps, steps)
        parts.append((field.at[levels], field_held.at[levels], field_out.at[levels]))
    loads = [
        pltpu.make_async_copy(src, held, in_sem.at[n]) for n, (src, held, _) in enumerate(parts)
    ]
    stores = [
        pltpu.make_async_copy(held, dst, out_sem.at[n]) for n, (_, held, dst) in enumerate(parts)
    ]
    for load in loads:
        load.start()
    for load, store in zip(loads, stores):
        load.wait()
        store.start()
    for store in stores:
        store.wait()


def per_device(ce, cn, cells, misfit, kern, ens, psrc, pdst, taper, var):
    hbm = pl.BlockSpec(memory_space=pl.ANY)
    tile = (TLAT, TLON)
    field, prior = pl.pallas_call(
        kernel,
        out_shape=(
            jax.ShapeDtypeStruct((LEV,) + tile, F32),
            jax.ShapeDtypeStruct(tile, F32),
        ),
        in_specs=[hbm] * 10,
        out_specs=(hbm, hbm),
        scratch_shapes=[
            pltpu.VMEM((8, 128), I32),
            pltpu.VMEM((FIELDS, 8, 128), F32),
            pltpu.SMEM((LEV,), F32),
            pltpu.VMEM((8, 128), I32),
            pltpu.VMEM((8, 128), I32),
            pltpu.VMEM((8, 128), F32),
            pltpu.VMEM(tile, F32),
            pltpu.VMEM((LEV,) + tile, F32),
            pltpu.VMEM((LEV, TLAT + 8, TLON), F32),
            pltpu.VMEM((LEV,) + tile, F32),
            pltpu.VMEM((LEV,) + tile, F32),
            pltpu.VMEM((LEV,) + tile, F32),
            pltpu.VMEM((LEV, ROWS, TLON), F32),
            pltpu.VMEM((LEV,) + tile, BF16),
            pltpu.VMEM((LEV,) + tile, F32),
            pltpu.VMEM((MEM,) + tile, BF16),
            pltpu.VMEM((EXT, ROWS, TLON), F32),
            pltpu.VMEM((ROWS, TLON), F32),
            pltpu.VMEM((ROWS, TLON), F32),
            pltpu.VMEM(tile, F32),
            pltpu.VMEM(tile, F32),
            pltpu.VMEM(tile, F32),
            pltpu.VMEM(tile, F32),
            pltpu.VMEM((LEV, TLON), F32),
            pltpu.VMEM((LEV, TLON), F32),
            pltpu.VMEM((5,) + tile, F32),
        ]
        + [pltpu.VMEM((ROUNDS, GROUPS) + tile, F32) for _ in range(3)]
        + [pltpu.VMEM((256, 256), BF16) for _ in range(3)]
        + [pltpu.VMEM((128, 128), BF16)]
        + [pltpu.VMEM((ROUNDS, GROUPS, KG, TLON), F32) for _ in range(4)]
        + [
            pltpu.VMEM((NLON, 2, 8, 128), F32),
            pltpu.VMEM((NLON, 2, 8, 128), F32),
            pltpu.VMEM((NLAT, 2, 16, 128), F32),
            pltpu.VMEM((NLAT, 2, 16, 128), F32),
            pltpu.VMEM((3, 64, 128), F32),
            pltpu.VMEM((256, 512), F32),
            pltpu.VMEM((2, 256, 512), BF16),
            pltpu.VMEM((256 * 8, TLON), F32),
            pltpu.VMEM((8, 256), F32),
            pltpu.VMEM((2, 64, 8, 256), F32),
            pltpu.VMEM((4, MEM, TLON), F32),
            pltpu.VMEM(tile, F32),
            pltpu.SemaphoreType.DMA((12,)),
            pltpu.SemaphoreType.DMA((GROUPS + 1,)),
            pltpu.SemaphoreType.DMA((COPIES,)),
            pltpu.SemaphoreType.DMA((COPIES,)),
        ],
        compiler_params=pltpu.CompilerParams(
            collective_id=0, has_side_effects=True, vmem_limit_bytes=60 * 1024 * 1024
        ),
    )(
        ce, cn, cells.reshape(8, 128), misfit.reshape(FIELDS, 8, 128), kern, ens,
        psrc.reshape(8, 128), pdst.reshape(8, 128), taper.reshape(8, 128), var,
    )
    return pl.pallas_call(
        hand_over,
        out_shape=(
            jax.ShapeDtypeStruct((LEV,) + tile, F32),
            jax.ShapeDtypeStruct(tile, F32),
        ),
        in_specs=[hbm] * 2,
        out_specs=(hbm, hbm),
        scratch_shapes=[
            pltpu.VMEM((LEV,) + tile, F32),
            pltpu.VMEM(tile, F32),
            pltpu.SemaphoreType.DMA((PIECES + 1,)),
            pltpu.SemaphoreType.DMA((PIECES + 1,)),
        ],
        compiler_params=pltpu.CompilerParams(vmem_limit_bytes=60 * 1024 * 1024),
    )(field, prior)


def solution(mesh):
    in_specs = (
        P(None, "lat", "lon"),
        P(None, "lat", "lon"),
        P("lat", "lon", None),
        P(None, "lat", "lon", None),
        P(),
        P(None, "lat", "lon"),
        P(("lon", "lat")),
        P(("lon", "lat")),
        P(("lon", "lat")),
        P("lat", "lon"),
    )
    out_specs = (P(None, "lat", "lon"), P("lat", "lon"))
    return jax.shard_map(
        per_device, mesh=mesh, in_specs=in_specs, out_specs=out_specs, check_vma=False
    )
```
